32 devices in a mesh: leaf: 8 (over z, x), vec: 4 (over y, core).
Axes of the slice: x: 2, y: 2, z: 4, core: 2. Of those that a mesh axis runs over, the one named last changes fastest.
Arguments:
- panels: float32 [32, 65536], P('vec', 'leaf'), may hold values from -6 to 6
- near_tiles: float32 [512, 4, 128, 128], P('leaf', None, 'vec'), may hold values from -0.25 to 0.25
- near_cols: int32 [512, 4], P('leaf'), may hold values from 0 to 511, as said below
- leaf_order: int32 [512, 128], P('leaf'), may hold values from 0 to 127, each once within a row
- leaf_basis: float32 [512, 64, 128], P('leaf'), may hold values from -0.5 to 0.5
- local_mats: float32 [8, 63, 64, 128], P('leaf'), may hold values from -0.75 to 0.75
- local_flags: int32 [8, 63], P('leaf'), may hold values 0 or 1
- cross_coupling: float32 [6, 64, 64], replicated, may hold values from -0.75 to 0.75
- cross_transfer: float32 [4, 64, 64], replicated, may hold values from -0.75 to 0.75
- cross_flags: int32 [6], replicated, may hold values 0 or 1
Outputs:
- product: float32 [32, 65536], P('vec', 'leaf')
The draws below stay inside these ranges and needn't reach their ends.
Inputs may be any that keep to these rules, and one draw needn't show every extreme that they name: `near_cols`: every entry of row i names a leaf within 8 leaves of leaf i. `leaf_order`: each row is a permutation of 0 to 127.
All inputs are finite; a program needn't handle non-finite values. No bound on the sum of `local_flags` on one device may be relied on, other than what follows from the above.
Results may differ from the reference program's by a relative error of at most 0.00022.
Values sent between devices are 32-bit elements; how exact they have to be, the bound alone decides.
A program may use at most 64 MiB of HBM per device.

```python
import math
import jax
import jax.numpy as jnp
from jax import lax

M = 128
K = 64
R = 32
NEAR = 4
W = 8
LEAF_DEV = 64
LEAVES = 512
PANELS = 65536
LOCAL_DEPTH = 6
LEAF_DEPTH = 3
N_LEAF = 8


def draw_near_cols(key, part):
    row_ids = jnp.arange(LEAVES, dtype=jnp.int32)[:, None]
    offsets = jax.random.randint(key, (LEAVES, NEAR), -W, W + 1, dtype=jnp.int32)
    offsets = offsets.at[0, 0].set(W).at[LEAVES - 1, 0].set(-W)
    return jnp.clip(row_ids + offsets, 0, LEAVES - 1).astype(jnp.int32)


def touch_ends(values, key, smallest, largest):
    spot = [jax.random.randint(jax.random.fold_in(key, axis), (), 0, length) for axis, length in enumerate(values.shape)]
    widest = values.shape.index(max(values.shape))
    next_to = spot[:widest] + [(spot[widest] + 1) % values.shape[widest]] + spot[widest + 1:]
    return values.at[tuple(spot)].set(smallest).at[tuple(next_to)].set(largest)


def steps_of(stream_key, shape, shards, low, top_value):
    def one(axis_at, blocks):
        draws = jax.random.uniform(jax.random.fold_in(jax.random.fold_in(stream_key, 6), axis_at), (blocks,), jnp.float32, low / len(shards), top_value / len(shards))
        return jnp.repeat(jnp.exp(draws), shape[axis_at] // blocks).reshape((-1,) + (1,) * (len(shape) - axis_at - 1))

    factor_of = one(*shards[0])
    for cut in shards[1:]:
        factor_of = factor_of * one(*cut)
    return factor_of


def scatter_about(stream_key, extent, scale, limit, split=(), kind=jnp.bfloat16):
    values = jax.random.normal(stream_key, extent, jnp.float32) * scale
    if len(split) > 0:
        values = steps_of(stream_key, extent, split, -0.22, 0.18) * values
    return jnp.clip(values, min=-limit, max=limit).astype(kind)


def setup_inputs(seed: int = 0) -> dict:
    splits = jax.random.split(jax.random.key(seed), 11)
    panels = scatter_about(splits[0], (R, PANELS), 1.0, 6.0, ((0, 4), (1, 8)), jnp.float32)
    near_tiles = scatter_about(splits[1], (LEAVES, NEAR, M, M), (NEAR * M) ** -0.5, 0.25, ((0, 8), (2, 4)), jnp.float32)
    near_cols = draw_near_cols(jax.random.fold_in(splits[10], 71), 0)
    leaf_order = jax.vmap(lambda own: jax.random.permutation(own, M))(jax.random.split(splits[3], LEAVES)).reshape((LEAVES, M)).astype(jnp.int32)
    leaf_basis = scatter_about(splits[4], (LEAVES, K, M), M ** -0.5, 0.5, ((0, 8),), jnp.float32)
    local_mats = scatter_about(splits[5], (LEAVES // LEAF_DEV, LEAF_DEV - 1, K, 2 * K), K ** -0.5, 0.75, ((0, 8),), jnp.float32)
    local_flags = touch_ends((jax.random.randint(splits[6], (LEAVES // LEAF_DEV, LEAF_DEV - 1), 0, 4) < 3).astype(jnp.int32), jax.random.fold_in(splits[6], 1), 0, 1)
    cross_coupling = scatter_about(splits[7], (LEAVES // LEAF_DEV - 2, K, K), K ** -0.5, 0.75, (), jnp.float32)
    cross_transfer = scatter_about(splits[8], (LEAVES // LEAF_DEV - 4, K, K), K ** -0.5, 0.75, (), jnp.float32)
    cross_flags = touch_ends((jax.random.randint(splits[9], (LEAVES // LEAF_DEV - 2,), 0, 4) < 3).astype(jnp.int32), jax.random.fold_in(splits[9], 1), 0, 1)
    return dict(panels=panels, near_tiles=near_tiles, near_cols=near_cols, leaf_order=leaf_order, leaf_basis=leaf_basis, local_mats=local_mats, local_flags=local_flags, cross_coupling=cross_coupling, cross_transfer=cross_transfer, cross_flags=cross_flags)


precise = lax.Precision.HIGHEST
root_half = 1.0 / math.sqrt(2.0)

def swap_pairs(nodes):
    halves = nodes.reshape((nodes.shape[0] // 2, 2) + nodes.shape[1:])
    return halves[:, ::-1].reshape(nodes.shape)

def level_blocks(tree_level, local_mats, local_flags, cross_coupling, cross_transfer, cross_flags):
    if tree_level <= LOCAL_DEPTH:
        per_device = LEAF_DEV // 2 ** tree_level
        first_node = LEAF_DEV - LEAF_DEV // 2 ** (tree_level - 1)
        blocks = local_mats[:, first_node:first_node + per_device].reshape(N_LEAF * per_device, K, 2 * K)
        admits = local_flags[:, first_node:first_node + per_device].reshape(N_LEAF * per_device)
        return (blocks[:, :, :K], blocks[:, :, K:], admits)
    cross_level = tree_level - LOCAL_DEPTH
    node_count = N_LEAF // 2 ** cross_level
    first_node = N_LEAF - N_LEAF // 2 ** (cross_level - 1)
    couplings = cross_coupling[first_node:first_node + node_count]
    admits = cross_flags[first_node:first_node + node_count]
    if cross_level <= LEAF_DEPTH - 2:
        return (couplings, cross_transfer[first_node:first_node + node_count], admits)
    return (couplings, couplings, admits)

def reference(panels, near_tiles, near_cols, leaf_order, leaf_basis, local_mats, local_flags, cross_coupling, cross_transfer, cross_flags):
    rhs_count = panels.shape[0]
    order_full = jnp.broadcast_to(leaf_order[None], (rhs_count, LEAVES, M))
    ordered = jnp.take_along_axis(panels.reshape(rhs_count, LEAVES, M), order_full, axis=2)

    def near_block(block_pair):
        tile_block, columns = block_pair
        sources = ordered[:, columns]
        return jnp.einsum('lnqp,slnp->slq', tile_block, sources, precision=precise)
    blocks = lax.map(near_block, (near_tiles.reshape(N_LEAF, LEAF_DEV, NEAR, M, M), near_cols.reshape(N_LEAF, LEAF_DEV, NEAR)))
    near_field = jnp.transpose(blocks, (1, 0, 2, 3)).reshape(rhs_count, LEAVES, M)
    leaf_skel = jnp.einsum('lkp,slp->lsk', leaf_basis, ordered, precision=precise)
    skeleton = leaf_skel.reshape(LEAVES // 2, 2, rhs_count, K).sum(axis=1) * root_half
    top_level = LOCAL_DEPTH + LEAF_DEPTH - 1
    coupled = []
    transfers = []
    for tree_level in range(1, top_level + 1):
        couplings, transfer, admits = level_blocks(tree_level, local_mats, local_flags, cross_coupling, cross_transfer, cross_flags)
        term = jnp.einsum('jkm,jsm->jsk', couplings, swap_pairs(skeleton), precision=precise)
        coupled.append(admits.astype(jnp.float32)[:, None, None] * term)
        transfers.append(transfer)
        if tree_level < top_level:
            lifted = jnp.einsum('jsk,jkm->jsm', skeleton, transfer, precision=precise)
            skeleton = lifted.reshape(lifted.shape[0] // 2, 2, rhs_count, K).sum(axis=1) * root_half
    downward = coupled[top_level - 1]
    for tree_level in range(top_level - 1, 0, -1):
        spread = jnp.repeat(downward, 2, axis=0)
        downward = coupled[tree_level - 1] + jnp.einsum('jkm,jsm->jsk', transfers[tree_level - 1], spread, precision=precise)
    far_field = jnp.einsum('lkp,lsk->slp', leaf_basis, jnp.repeat(downward, 2, axis=0), precision=precise)
    combined = near_field + far_field
    inverse = jnp.argsort(leaf_order, axis=1).astype(jnp.int32)
    restored = jnp.take_along_axis(combined, jnp.broadcast_to(inverse[None], (rhs_count, LEAVES, M)), axis=2)
    return restored.reshape(rhs_count, PANELS)
```

```python
import functools
import math

import jax
import jax.numpy as jnp
from jax import lax
from jax.experimental import pallas as pl
from jax.experimental.pallas import tpu as pltpu
from jax.sharding import PartitionSpec as P

W = 8
f32 = jnp.float32
bf16 = jnp.bfloat16
root_half = 1.0 / math.sqrt(2.0)
MESH = pl.DeviceIdType.MESH
NN = (((1,), (0,)), ((), ()))
NT = (((1,), (1,)), ((), ()))


def halves(x):
    high = x.astype(bf16).astype(f32)
    return high, x - high


def stacked(x):
    return jnp.concatenate(halves(x), axis=0).astype(bf16)


def split(w):
    high = w.astype(bf16)
    return high, (w - high.astype(f32)).astype(bf16)


def dot_nt(x, w):
    rows = x.shape[0]
    lhs = stacked(x)
    r = lax.dot_general(
        jnp.concatenate([lhs, lhs], axis=1),
        jnp.concatenate(split(w), axis=1),
        NT,
        preferred_element_type=f32,
    )
    return r[:rows] + r[rows:]


def dot_nn(x, w):
    rows, cols = x.shape[0], w.shape[1]
    r = lax.dot_general(
        stacked(x), jnp.concatenate(split(w), axis=1), NN, preferred_element_type=f32
    )
    r = r[:, :cols] + r[:, cols:]
    return r[:rows] + r[rows:]


def hot_of(order_row):
    size = order_row.shape[1]
    rows = lax.broadcasted_iota(jnp.int32, (size, size), 0)
    return jnp.where(rows == order_row, 1.0, 0.0).astype(bf16)


def main_kernel(
    n_leaf,
    n_vec,
    panels_hbm,
    order_hbm,
    cols_hbm,
    flags_hbm,
    cross_flags_hbm,
    cross_c_hbm,
    cross_e_hbm,
    tiles_hbm,
    basis_hbm,
    mats_hbm,
    out_ref,
    panels,
    order,
    cols_ref,
    flags_ref,
    cross_flags_ref,
    cross_c_ref,
    cross_e_ref,
    tiles,
    basis,
    mats,
    ext,
    xs,
    tb,
    hp,
    zp,
    pay,
    hx,
    nout,
    near,
    far,
    inverse,
    load_sem,
    own_send,
    own_recv,
    gather_send,
    gather_recv,
    spread_send,
    spread_recv,
    halo_send,
    halo_recv,
    rim_send,
    rim_recv,
    pay_send,
    pay_recv,
    near_send,
    near_recv,
):
    leaves, size = order.shape
    rank = 64
    slots = tiles.shape[1]
    piece = tiles.shape[2]
    groups = leaves // n_vec
    li = lax.axis_index("leaf")
    vi = lax.axis_index("vec")
    loads = [
        pltpu.make_async_copy(src, dst, load_sem.at[i])
        for i, (src, dst) in enumerate(
            [
                (panels_hbm, panels),
                (order_hbm, order),
                (basis_hbm, basis),
                (mats_hbm, mats),
                (tiles_hbm, tiles),
                (cols_hbm, cols_ref),
                (flags_hbm, flags_ref),
                (cross_flags_hbm, cross_flags_ref),
                (cross_c_hbm, cross_c_ref),
                (cross_e_hbm, cross_e_ref),
            ]
        )
    ]
    for c in loads:
        c.start()
    load_p, load_o, load_b, load_m, load_t = loads[:5]
    small = loads[5:]

    barrier = pltpu.get_barrier_semaphore()
    greeted = 0
    for d in range(1, n_vec):
        pl.semaphore_signal(
            barrier, inc=1, device_id=(li, lax.rem(vi + d, n_vec)), device_id_type=MESH
        )
        greeted += 1
    for d in range(1, n_leaf):
        pl.semaphore_signal(
            barrier, inc=1, device_id=(lax.rem(li + d, n_leaf), vi), device_id_type=MESH
        )
        greeted += 1

    assert n_vec == 4
    beside = vi + 1 - 2 * lax.rem(vi, 2)
    across = lax.rem(vi + 2, n_vec)
    here = vi - lax.rem(vi, 2)
    there = lax.rem(here + 2, n_vec)
    has_left = li > 0
    has_right = li < n_leaf - 1
    inner = (leaves - 2 * W) // 3
    chunks = [(0, W), (leaves - W, W)] + [(W + k * inner, inner) for k in range(3)]

    own_copy = pltpu.make_async_remote_copy(
        src_ref=ext.at[vi, pl.ds(W, leaves)],
        dst_ref=ext.at[vi, pl.ds(W, leaves)],
        send_sem=own_send,
        recv_sem=own_recv,
        device_id=(li, beside),
        device_id_type=MESH,
    )

    def gather_copy(k):
        block = ext.at[vi, pl.ds(W + chunks[k][0], chunks[k][1])]
        return pltpu.make_async_remote_copy(
            src_ref=block,
            dst_ref=block,
            send_sem=gather_send.at[k],
            recv_sem=gather_recv.at[k],
            device_id=(li, across),
            device_id_type=MESH,
        )

    def spread_copy(k):
        block = ext.at[across, pl.ds(W + chunks[k][0], chunks[k][1])]
        return pltpu.make_async_remote_copy(
            src_ref=block,
            dst_ref=block,
            send_sem=spread_send.at[k],
            recv_sem=spread_recv.at[k],
            device_id=(li, beside),
            device_id_type=MESH,
        )

    rims = (0, leaves + W)
    sends = (has_right, has_left)
    takes = (has_left, has_right)

    def halo_copy(side, kind):
        vec = vi if kind == 0 else across
        target = jnp.minimum(li + 1, n_leaf - 1) if side == 0 else jnp.maximum(li - 1, 0)
        return pltpu.make_async_remote_copy(
            src_ref=ext.at[vec, pl.ds(leaves if side == 0 else W, W)],
            dst_ref=ext.at[vec, pl.ds(rims[side], W)],
            send_sem=halo_send.at[side, kind],
            recv_sem=halo_recv.at[side, kind],
            device_id=(target, vi),
            device_id_type=MESH,
        )

    def rim_copy(side, kind):
        block = ext.at[vi if kind == 0 else across, pl.ds(rims[side], W)]
        return pltpu.make_async_remote_copy(
            src_ref=block,
            dst_ref=block,
            send_sem=rim_send.at[side, kind],
            recv_sem=rim_recv.at[side, kind],
            device_id=(li, beside),
            device_id_type=MESH,
        )

    gathers = [gather_copy(k) for k in range(len(chunks))]
    spreads = [spread_copy(k) for k in range(len(chunks))]
    halos = [[halo_copy(side, kind) for side in range(2)] for kind in range(2)]
    rim_copies = [[rim_copy(side, kind) for side in range(2)] for kind in range(2)]

    def both(kind, copies, conditions, act):
        for side in range(2):
            @pl.when(conditions[side])
            def _(side=side):
                act(copies[kind][side])

    lane = lax.broadcasted_iota(jnp.int32, (8, 2 * rank), 1)
    low = lane < rank

    def swap(x):
        return pltpu.roll(x, rank, 1)

    load_p.wait()
    load_o.wait()

    def order_body(i, carry):
        for u in range(32):
            leaf = i * 32 + u
            x = panels[:, pl.ds(pl.multiple_of(leaf * size, size), size)]
            spots = jnp.broadcast_to(order[pl.ds(leaf, 1), :], x.shape)
            ext[vi, W + leaf] = jnp.take_along_axis(x, spots, axis=1)
        return carry

    lax.fori_loop(0, leaves // 32, order_body, 0)
    load_b.wait()

    def skel_body(i, carry):
        for w in range(8):
            t = i * 8 + w
            sums = []
            for u in range(2):
                pair = t * 2 + u
                x = ext[vi, pl.ds(W + pair * 2, 2)].reshape(16, 128)
                wt = basis[pl.ds(pl.multiple_of(pair * 128, 128), 128), :]
                r = dot_nt(x, wt)
                sums.append((r[:8], r[8:]))
            even = sums[0][0] + swap(sums[0][1])
            odd = swap(sums[1][0]) + sums[1][1]
            hp[t] = jnp.where(low, even, odd) * root_half
        return carry

    lax.fori_loop(0, leaves // 32, skel_body, 0)
    load_m.wait()

    def mat_pair(q):
        return mats[pl.ds(pl.multiple_of(q * 128, 128), 128), :]

    def up(off, nxt, t):
        r0 = dot_nn(hp[off + 2 * t], mat_pair(off + 2 * t))
        r1 = dot_nn(hp[off + 2 * t + 1], mat_pair(off + 2 * t + 1))
        hp[nxt + t] = jnp.where(low, swap(r0), r1) * root_half

    pairs = leaves // 4
    offs = []
    off = 0
    while pairs >= 1:
        offs.append((off, pairs))
        off += pairs
        pairs //= 2
    for (a, count), (b, half) in zip(offs[:-1], offs[1:]):
        for t in range(half):
            up(a, b, t)
    last = offs[-1][0]
    r = dot_nn(hp[last], mat_pair(last))
    skel = swap(r) * root_half
    top = mats[pl.ds((last + 1) * 128, rank), :]
    lift = dot_nn(skel[:, :rank], top)
    pay[li] = jnp.where(low, skel, lift)

    def pay_copy(d):
        return pltpu.make_async_remote_copy(
            src_ref=pay.at[li],
            dst_ref=pay.at[li],
            send_sem=pay_send.at[d],
            recv_sem=pay_recv.at[n_leaf - d],
            device_id=(lax.rem(li + d, n_leaf), vi),
            device_id_type=MESH,
        )

    pays = [pay_copy(d) for d in range(1, n_leaf)]

    pl.semaphore_wait(barrier, greeted)
    for c in gathers:
        c.start()
    own_copy.start()
    both(0, halos, sends, lambda c: c.start())
    for c in pays:
        c.start()

    counts = lax.broadcasted_iota(jnp.int32, (8, 128), 1).astype(f32).astype(bf16)

    def inverse_body(i, carry):
        for w in range(16):
            leaf = i * 16 + w
            hot = hot_of(order[pl.ds(leaf, 1), :])
            inverse[leaf] = lax.dot_general(counts, hot, NT, preferred_element_type=f32)
        return carry

    lax.fori_loop(0, leaves // 16, inverse_body, 0)

    def split_span(side, first, count):
        block = here if side == 0 else there

        def body(i, carry):
            for w in range(8):
                e = first + i * 8 + w
                x = ext[pl.ds(block, 2), e].reshape(16, 128)
                xs[side, e] = stacked(x)
            return carry

        lax.fori_loop(0, count // 8, body, 0)

    for c in small:
        c.wait()
    own_copy.wait_recv()
    split_span(0, W, leaves)
    load_t.wait()
    base = li * leaves - W

    def place(leaf, n):
        return jnp.clip(cols_ref[n, leaf] - base, 0, leaves + 2 * W - 1)

    def near_group(side, g):
        outs = []
        for w in range(n_vec):
            leaf = g * n_vec + w
            x = jnp.concatenate([xs[side, place(leaf, n)] for n in range(slots)], axis=1)
            if side == 0:
                t = jnp.concatenate([stacked(tiles[leaf, n]) for n in range(slots)], axis=1)
                tb[leaf] = t
            else:
                t = tb[leaf]
            r = lax.dot_general(x, t, NT, preferred_element_type=f32)
            r = r[:16] + r[16:]
            outs.append(r[:, :piece] + r[:, piece:])
        block = here if side == 0 else there
        nout[pl.ds(block, 2), g] = jnp.concatenate(outs, axis=1).reshape(2, 8, n_vec * piece)

    def near_span(side, first, count):
        def body(i, carry):
            for w in range(4):
                near_group(side, first + i * 4 + w)
            return carry

        lax.fori_loop(0, count // 4, body, 0)
        for g in range(first + count // 4 * 4, first + count):
            near_group(side, g)

    edge = W // n_vec
    middle = groups - 2 * edge
    near_span(0, edge, middle // 2)
    gathers[0].wait_recv()
    gathers[1].wait_recv()
    spreads[0].start()
    spreads[1].start()
    both(1, halos, sends, lambda c: c.start())
    both(0, halos, takes, lambda c: c.wait_recv())
    both(0, rim_copies, takes, lambda c: c.start())
    near_span(0, edge + middle // 2, middle - middle // 2)
    gathers[2].wait_recv()
    spreads[2].start()
    both(0, rim_copies, takes, lambda c: c.wait_recv())
    split_span(0, 0, W)
    split_span(0, leaves + W, W)
    near_span(0, 0, edge)
    near_span(0, groups - edge, edge)

    def near_copy(d, part, first, count):
        u = lax.rem(vi + d, n_vec) if d == 2 else (beside if d == 1 else 3 - vi)
        span = pl.ds(first, count)
        return pltpu.make_async_remote_copy(
            src_ref=nout.at[u, span],
            dst_ref=near.at[vi, span],
            send_sem=near_send.at[d, part],
            recv_sem=near_recv.at[d, part],
            device_id=(li, u),
            device_id_type=MESH,
        )

    nears = [near_copy(1, 0, 0, groups)]
    nears[0].start()
    keep = pltpu.make_async_copy(nout.at[vi], near.at[vi], near_send.at[0, 0])
    keep.start()
    both(1, halos, takes, lambda c: c.wait_recv())
    both(1, rim_copies, takes, lambda c: c.start())
    gathers[3].wait_recv()
    spreads[3].start()

    def near_part(part, first, count):
        near_span(1, first, count)
        for d in (2, 3):
            c = near_copy(d, part, first, count)
            c.start()
            nears.append(c)

    step = middle // 3
    for k in range(3):
        spreads[k].wait_recv()
        split_span(1, W + chunks[k][0], chunks[k][1])
    spreads[3].wait_recv()
    split_span(1, W + chunks[3][0], chunks[3][1])
    near_part(0, edge, step)
    gathers[4].wait_recv()
    spreads[4].start()
    spreads[4].wait_recv()
    split_span(1, W + chunks[4][0], chunks[4][1])
    near_part(1, edge + step, step)
    near_part(2, edge + 2 * step, step)
    both(1, rim_copies, takes, lambda c: c.wait_recv())
    split_span(1, 0, W)
    split_span(1, leaves + W, W)
    near_part(3, 0, edge)
    near_part(4, groups - edge, edge)

    for c in pays:
        c.wait_recv()
    depth = n_leaf.bit_length() - 1

    def cross_at(c):
        return n_leaf - (n_leaf >> (c - 1))

    lifts = [pay[j] for j in range(n_leaf)]
    at = 0
    starts = {}
    for c in range(1, depth):
        nodes = [
            (lifts[2 * j] + lifts[2 * j + 1]) * root_half for j in range(len(lifts) // 2)
        ]
        nodes = [swap(x) if c == 1 else x for x in nodes]
        starts[c] = at
        for j, x in enumerate(nodes):
            hx[at + j] = x
        at += len(nodes)
        if c < depth - 1:
            lifts = []
            for j, x in enumerate(nodes):
                y = dot_nn(x[:, :rank], cross_e_ref[cross_at(c) + j])
                lifts.append(jnp.concatenate([y, y], axis=1))
    z = None
    for c in range(depth - 1, 0, -1):
        node = li >> c
        sibling = node + 1 - 2 * lax.rem(node, 2)
        spot = cross_at(c) + node
        a = cross_flags_ref[spot].astype(f32)
        g = dot_nt(a * hx[starts[c] + sibling][:, :rank], cross_c_ref[spot])
        z = g if z is None else g + dot_nt(z, cross_e_ref[spot])
    sibling = li + 1 - 2 * lax.rem(li, 2)
    a = flags_ref[0, 2 * (last + 1)].astype(f32)
    x = jnp.where(low, a * pay[sibling], jnp.concatenate([z, z], axis=1))
    z = dot_nt(x, top)
    z = jnp.concatenate([z, z], axis=1)

    def down(q, parent):
        h = hp[q]
        a0 = flags_ref[0, 2 * q].astype(f32)
        a1 = flags_ref[0, 2 * q + 1].astype(f32)
        x0 = jnp.where(low, a0 * swap(h), parent)
        x1 = jnp.where(low, a1 * h, parent)
        r = dot_nt(jnp.concatenate([x0, x1], axis=0), mat_pair(q))
        zp[q] = jnp.where(low, r[:8], r[8:])

    down(last, z)
    for (a, count), (b, half) in list(zip(offs[:-1], offs[1:]))[::-1]:
        for t in range(half):
            p = zp[b + t]
            down(a + 2 * t, swap(p))
            down(a + 2 * t + 1, p)

    def far_body(i, carry):
        for w in range(8):
            t = i * 8 + w
            p = zp[t]
            s = swap(p)
            zero = jnp.zeros_like(p)
            for u in range(2):
                pair = 2 * t + u
                first, second = (p, s) if u == 0 else (s, p)
                x = jnp.concatenate(
                    [jnp.where(low, first, zero), jnp.where(low, zero, second)], axis=0
                )
                wt = basis[pl.ds(pl.multiple_of(pair * 128, 128), 128), :]
                r = dot_nn(x, wt)
                far[2 * pair] = r[:8]
                far[2 * pair + 1] = r[8:]
        return carry

    lax.fori_loop(0, leaves // 32, far_body, 0)
    keep.wait()
    for c in nears:
        c.wait_recv()

    block = lax.broadcasted_iota(jnp.int32, (8, size), 1) // piece

    def group(g):
        parts = [near[v, g] for v in range(n_vec)]
        for u in range(n_vec):
            leaf = g * n_vec + u
            total = parts[0] if u == 0 else pltpu.roll(parts[0], (size - u * piece), 1)
            for v in range(1, n_vec):
                shift = ((v - u) * piece) % size
                moved = parts[v] if shift == 0 else pltpu.roll(parts[v], shift, 1)
                total = jnp.where(block == v, moved, total)
            spots = inverse[leaf].astype(jnp.int32)
            out_ref[:, pl.ds(pl.multiple_of(leaf * size, size), size)] = jnp.take_along_axis(
                total + far[leaf], spots, axis=1
            )

    def restore_body(i, carry):
        for w in range(8):
            group(i * 8 + w)
        return carry

    lax.fori_loop(0, groups // 8, restore_body, 0)
    for c in nears + pays + gathers + spreads + [own_copy]:
        c.wait_send()
    for kind in range(2):
        both(kind, halos, sends, lambda c: c.wait_send())
        both(kind, rim_copies, takes, lambda c: c.wait_send())


def local(
    panels,
    near_tiles,
    near_cols,
    leaf_order,
    leaf_basis,
    local_mats,
    local_flags,
    cross_coupling,
    cross_transfer,
    cross_flags,
):
    rows = panels.shape[0]
    leaves, rank, size = leaf_basis.shape
    n_leaf = lax.axis_size("leaf")
    n_vec = lax.axis_size("vec")
    piece = near_tiles.shape[2]
    slots = near_tiles.shape[1]
    vmem = pl.BlockSpec(memory_space=pltpu.VMEM)
    hbm = pl.BlockSpec(memory_space=pl.ANY)
    basis2 = leaf_basis.reshape(leaves * rank, size)
    mats2 = local_mats.reshape(local_mats.shape[1] * rank, 2 * rank)
    groups = leaves // n_vec
    dma = pltpu.SemaphoreType.DMA
    return pl.pallas_call(
        functools.partial(main_kernel, n_leaf, n_vec),
        out_shape=jax.ShapeDtypeStruct(panels.shape, f32),
        in_specs=[hbm] * 10,
        out_specs=vmem,
        scratch_shapes=[
            pltpu.VMEM(panels.shape, f32),
            pltpu.VMEM(leaf_order.shape, jnp.int32),
            pltpu.SMEM(near_cols.shape[::-1], jnp.int32),
            pltpu.SMEM(local_flags.shape, jnp.int32),
            pltpu.SMEM(cross_flags.shape, jnp.int32),
            pltpu.VMEM(cross_coupling.shape, f32),
            pltpu.VMEM(cross_transfer.shape, f32),
            pltpu.VMEM(near_tiles.shape, f32),
            pltpu.VMEM(basis2.shape, f32),
            pltpu.VMEM(mats2.shape, f32),
            pltpu.VMEM((n_vec, leaves + 2 * W, rows, size), f32),
            pltpu.VMEM((2, leaves + 2 * W, n_vec * rows, size), bf16),
            pltpu.VMEM((leaves, 2 * piece, slots * size), bf16),
            pltpu.VMEM((leaves // 2, rows, size), f32),
            pltpu.VMEM((leaves // 2, rows, size), f32),
            pltpu.VMEM((n_leaf, rows, 2 * rank), f32),
            pltpu.VMEM((n_leaf, rows, 2 * rank), f32),
            pltpu.VMEM((n_vec, groups, rows, size), f32),
            pltpu.VMEM((n_vec, groups, rows, size), f32),
            pltpu.VMEM((leaves, rows, size), f32),
            pltpu.VMEM((leaves, rows, size), f32),
            dma((10,)),
            dma,
            dma,
            dma((5,)),
            dma((5,)),
            dma((5,)),
            dma((5,)),
            dma((2, 2)),
            dma((2, 2)),
            dma((2, 2)),
            dma((2, 2)),
            dma((n_leaf,)),
            dma((n_leaf,)),
            dma((n_vec, 5)),
            dma((n_vec, 5)),
        ],
        compiler_params=pltpu.CompilerParams(
            collective_id=0, has_side_effects=True, vmem_limit_bytes=62 * 1024 * 1024
        ),
        name="tree",
    )(
        panels,
        leaf_order,
        near_cols.T,
        local_flags,
        cross_flags,
        cross_coupling,
        cross_transfer,
        near_tiles,
        basis2,
        mats2,
    )


def solution(mesh):
    return jax.shard_map(
        local,
        mesh=mesh,
        in_specs=(
            P("vec", "leaf"),
            P("leaf", None, "vec", None),
            P("leaf", None),
            P("leaf", None),
            P("leaf", None, None),
            P("leaf", None, None, None),
            P("leaf", None),
            P(),
            P(),
            P(),
        ),
        out_specs=P("vec", "leaf"),
        check_vma=False,
    )
```

```python
import functools
import math

import jax
import jax.numpy as jnp
from jax import lax
from jax.experimental import pallas as pl
from jax.experimental.pallas import tpu as pltpu
from jax.sharding import PartitionSpec as P

W = 8
f32 = jnp.float32
bf16 = jnp.bfloat16
root_half = 1.0 / math.sqrt(2.0)
MESH = pl.DeviceIdType.MESH
NN = (((1,), (0,)), ((), ()))
NT = (((1,), (1,)), ((), ()))


def halves(x):
    high = x.astype(bf16).astype(f32)
    return high, x - high


def stacked(x):
    return jnp.concatenate(halves(x), axis=0).astype(bf16)


def split(w):
    high = w.astype(bf16)
    return high, (w - high.astype(f32)).astype(bf16)


def dot_nt(x, w):
    rows = x.shape[0]
    lhs = stacked(x)
    r = lax.dot_general(
        jnp.concatenate([lhs, lhs], axis=1),
        jnp.concatenate(split(w), axis=1),
        NT,
        preferred_element_type=f32,
    )
    return r[:rows] + r[rows:]


def dot_nn(x, w):
    rows, cols = x.shape[0], w.shape[1]
    r = lax.dot_general(
        stacked(x), jnp.concatenate(split(w), axis=1), NN, preferred_element_type=f32
    )
    r = r[:, :cols] + r[:, cols:]
    return r[:rows] + r[rows:]


def hot_of(order_row):
    size = order_row.shape[1]
    rows = lax.broadcasted_iota(jnp.int32, (size, size), 0)
    return jnp.where(rows == order_row, 1.0, 0.0).astype(bf16)


def main_kernel(
    n_leaf,
    n_vec,
    panels_hbm,
    order_hbm,
    cols_hbm,
    flags_hbm,
    cross_flags_hbm,
    cross_c_hbm,
    cross_e_hbm,
    tiles_hbm,
    basis_hbm,
    mats_hbm,
    out_ref,
    panels,
    order,
    cols_ref,
    flags_ref,
    cross_flags_ref,
    cross_c_ref,
    cross_e_ref,
    tiles,
    basis,
    mats,
    ext,
    xs,
    tb,
    hp,
    zp,
    pay,
    hx,
    nout,
    near,
    far,
    inverse,
    load_sem,
    own_send,
    own_recv,
    gather_send,
    gather_recv,
    spread_send,
    spread_recv,
    halo_send,
    halo_recv,
    rim_send,
    rim_recv,
    pay_send,
    pay_recv,
    near_send,
    near_recv,
):
    leaves, size = order.shape
    rank = 64
    slots = tiles.shape[1]
    piece = tiles.shape[2]
    groups = leaves // n_vec
    li = lax.axis_index("leaf")
    vi = lax.axis_index("vec")
    loads = [
        pltpu.make_async_copy(src, dst, load_sem.at[i])
        for i, (src, dst) in enumerate(
            [
                (panels_hbm, panels),
                (order_hbm, order),
                (basis_hbm, basis),
                (mats_hbm, mats),
                (tiles_hbm, tiles),
                (cols_hbm, cols_ref),
                (flags_hbm, flags_ref),
                (cross_flags_hbm, cross_flags_ref),
                (cross_c_hbm, cross_c_ref),
                (cross_e_hbm, cross_e_ref),
            ]
        )
    ]
    load_p, load_o, load_b, load_m, load_t = loads[:5]
    small = loads[5:]
    for c in loads[:3]:
        c.start()

    barrier = pltpu.get_barrier_semaphore()
    for d in range(1, n_vec):
        pl.semaphore_signal(
            barrier, inc=1, device_id=(li, lax.rem(vi + d, n_vec)), device_id_type=MESH
        )
    for d in range(1, n_leaf):
        @pl.when(li + d < n_leaf)
        def _(d=d):
            pl.semaphore_signal(
                barrier, inc=1, device_id=(lax.rem(li + d, n_leaf), vi), device_id_type=MESH
            )
    load_m.start()
    for c in small:
        c.start()

    assert n_vec == 4
    beside = vi + 1 - 2 * lax.rem(vi, 2)
    across = lax.rem(vi + 2, n_vec)
    here = vi - lax.rem(vi, 2)
    there = lax.rem(here + 2, n_vec)
    has_left = li > 0
    has_right = li < n_leaf - 1
    chunks = [(0, W), (leaves - W, W)]
    at = W
    while at < leaves - W:
        wide = 2 * W if leaves - W - at > 2 * W else W
        chunks.append((at, wide))
        at += wide

    own_copy = pltpu.make_async_remote_copy(
        src_ref=ext.at[vi, pl.ds(W, leaves)],
        dst_ref=ext.at[vi, pl.ds(W, leaves)],
        send_sem=own_send,
        recv_sem=own_recv,
        device_id=(li, beside),
        device_id_type=MESH,
    )

    def gather_copy(k):
        block = ext.at[vi, pl.ds(W + chunks[k][0], chunks[k][1])]
        return pltpu.make_async_remote_copy(
            src_ref=block,
            dst_ref=block,
            send_sem=gather_send.at[k],
            recv_sem=gather_recv.at[k],
            device_id=(li, across),
            device_id_type=MESH,
        )

    def spread_copy(k):
        block = ext.at[across, pl.ds(W + chunks[k][0], chunks[k][1])]
        return pltpu.make_async_remote_copy(
            src_ref=block,
            dst_ref=block,
            send_sem=spread_send.at[k],
            recv_sem=spread_recv.at[k],
            device_id=(li, beside),
            device_id_type=MESH,
        )

    rims = (0, leaves + W)
    sends = (has_right, has_left)
    takes = (has_left, has_right)

    def halo_copy(side, kind):
        vec = vi if kind == 0 else across
        target = jnp.minimum(li + 1, n_leaf - 1) if side == 0 else jnp.maximum(li - 1, 0)
        return pltpu.make_async_remote_copy(
            src_ref=ext.at[vec, pl.ds(leaves if side == 0 else W, W)],
            dst_ref=ext.at[vec, pl.ds(rims[side], W)],
            send_sem=halo_send.at[side, kind],
            recv_sem=halo_recv.at[side, kind],
            device_id=(target, vi),
            device_id_type=MESH,
        )

    def rim_copy(side, kind):
        block = ext.at[vi if kind == 0 else across, pl.ds(rims[side], W)]
        return pltpu.make_async_remote_copy(
            src_ref=block,
            dst_ref=block,
            send_sem=rim_send.at[side, kind],
            recv_sem=rim_recv.at[side, kind],
            device_id=(li, beside),
            device_id_type=MESH,
        )

    gathers = [gather_copy(k) for k in range(len(chunks))]
    spreads = [spread_copy(k) for k in range(len(chunks))]
    halos = [[halo_copy(side, kind) for side in range(2)] for kind in range(2)]
    rim_copies = [[rim_copy(side, kind) for side in range(2)] for kind in range(2)]

    def begin(c):
        c.start()

    def landed(c):
        c.wait_recv()

    def one(side, kind, copies, conditions, act):
        @pl.when(conditions[side])
        def _():
            act(copies[kind][side])

    def both(kind, copies, conditions, act):
        for side in range(2):
            one(side, kind, copies, conditions, act)

    lane = lax.broadcasted_iota(jnp.int32, (8, 2 * rank), 1)
    low = lane < rank

    def swap(x):
        return pltpu.roll(x, rank, 1)

    load_p.wait()
    load_o.wait()

    def order_body(i, carry):
        for u in range(32):
            leaf = i * 32 + u
            x = panels[:, pl.ds(pl.multiple_of(leaf * size, size), size)]
            spots = jnp.broadcast_to(order[pl.ds(leaf, 1), :], x.shape)
            ext[vi, W + leaf] = jnp.take_along_axis(x, spots, axis=1)
        return carry

    lax.fori_loop(0, leaves // 32, order_body, 0)
    pl.semaphore_wait(barrier, n_vec - 1 + li)
    for c in gathers:
        c.start()
    own_copy.start()
    one(1, 0, halos, sends, begin)
    load_b.wait()
    load_t.start()

    def skel_body(i, carry):
        for w in range(8):
            t = i * 8 + w
            sums = []
            for u in range(2):
                pair = t * 2 + u
                x = ext[vi, pl.ds(W + pair * 2, 2)].reshape(16, 128)
                wt = basis[pl.ds(pl.multiple_of(pair * 128, 128), 128), :]
                r = dot_nt(x, wt)
                sums.append((r[:8], r[8:]))
            even = sums[0][0] + swap(sums[0][1])
            odd = swap(sums[1][0]) + sums[1][1]
            hp[t] = jnp.where(low, even, odd) * root_half
        return carry

    lax.fori_loop(0, leaves // 32, skel_body, 0)
    load_m.wait()

    def mat_pair(q):
        return mats[pl.ds(pl.multiple_of(q * 128, 128), 128), :]

    def up(off, nxt, t):
        r0 = dot_nn(hp[off + 2 * t], mat_pair(off + 2 * t))
        r1 = dot_nn(hp[off + 2 * t + 1], mat_pair(off + 2 * t + 1))
        hp[nxt + t] = jnp.where(low, swap(r0), r1) * root_half

    pairs = leaves // 4
    offs = []
    off = 0
    while pairs >= 1:
        offs.append((off, pairs))
        off += pairs
        pairs //= 2
    for (a, count), (b, half) in zip(offs[:-1], offs[1:]):
        for t in range(half):
            up(a, b, t)
    last = offs[-1][0]
    r = dot_nn(hp[last], mat_pair(last))
    skel = swap(r) * root_half
    top = mats[pl.ds((last + 1) * 128, rank), :]
    lift = dot_nn(skel[:, :rank], top)
    pay[li] = jnp.where(low, skel, lift)

    def pay_copy(d):
        return pltpu.make_async_remote_copy(
            src_ref=pay.at[li],
            dst_ref=pay.at[li],
            send_sem=pay_send.at[d],
            recv_sem=pay_recv.at[n_leaf - d],
            device_id=(lax.rem(li + d, n_leaf), vi),
            device_id_type=MESH,
        )

    pays = [pay_copy(d) for d in range(1, n_leaf)]

    for d in range(1, n_leaf):
        @pl.when(li + d >= n_leaf)
        def _(d=d):
            pays[d - 1].start()

    counts = lax.broadcasted_iota(jnp.int32, (8, 128), 1).astype(f32).astype(bf16)

    def inverse_body(i, carry):
        for w in range(16):
            leaf = i * 16 + w
            hot = hot_of(order[pl.ds(leaf, 1), :])
            inverse[leaf] = lax.dot_general(counts, hot, NT, preferred_element_type=f32)
        return carry

    lax.fori_loop(0, leaves // 16, inverse_body, 0)

    def split_span(side, first, count):
        block = here if side == 0 else there

        def body(i, carry):
            for w in range(8):
                e = first + i * 8 + w
                x = ext[pl.ds(block, 2), e].reshape(16, 128)
                xs[side, e] = stacked(x)
            return carry

        lax.fori_loop(0, count // 8, body, 0)

    for c in small:
        c.wait()
    own_copy.wait_recv()
    split_span(0, W, leaves)
    load_t.wait()
    base = li * leaves - W

    def place(leaf, n):
        return jnp.clip(cols_ref[n, leaf] - base, 0, leaves + 2 * W - 1)

    def near_group(side, g):
        outs = []
        for w in range(n_vec):
            leaf = g * n_vec + w
            x = jnp.concatenate([xs[side, place(leaf, n)] for n in range(slots)], axis=1)
            if side == 0:
                t = jnp.concatenate([stacked(tiles[leaf, n]) for n in range(slots)], axis=1)
                tb[leaf] = t
            else:
                t = tb[leaf]
            r = lax.dot_general(x, t, NT, preferred_element_type=f32)
            r = r[:16] + r[16:]
            outs.append(r[:, :piece] + r[:, piece:])
        block = here if side == 0 else there
        nout[pl.ds(block, 2), g] = jnp.concatenate(outs, axis=1).reshape(2, 8, n_vec * piece)

    def near_span(side, first, count):
        def body(i, carry):
            for w in range(4):
                near_group(side, first + i * 4 + w)
            return carry

        lax.fori_loop(0, count // 4, body, 0)
        for g in range(first + count // 4 * 4, first + count):
            near_group(side, g)

    edge = W // n_vec
    middle = groups - 2 * edge

    def pass_on(k):
        gathers[k].wait_recv()
        spreads[k].start()

    def take(k):
        spreads[k].wait_recv()
        split_span(1, W + chunks[k][0], chunks[k][1])

    pass_on(0)
    pass_on(1)
    one(1, 0, halos, takes, landed)
    one(0, 0, halos, sends, begin)
    both(1, halos, sends, begin)
    one(1, 0, rim_copies, takes, begin)
    near_span(0, edge, middle // 2)
    pass_on(2)
    near_span(0, edge + middle // 2, middle - middle // 2)
    pass_on(3)
    one(0, 0, halos, takes, landed)
    one(0, 0, rim_copies, takes, begin)
    take(0)
    take(1)
    take(2)
    both(1, halos, takes, landed)
    both(1, rim_copies, takes, begin)

    def near_copy(d, part, first, count):
        u = across if d == 2 else (beside if d == 1 else n_vec - 1 - vi)
        span = pl.ds(first, count)
        return pltpu.make_async_remote_copy(
            src_ref=nout.at[u, span],
            dst_ref=near.at[vi, span],
            send_sem=near_send.at[d, part],
            recv_sem=near_recv.at[d, part],
            device_id=(li, u),
            device_id_type=MESH,
        )

    nears = []
    parts = []

    def near_part(first):
        near_span(1, first, edge)
        batch = [near_copy(d, len(parts), first, edge) for d in (2, 3)]
        for c in batch:
            c.start()
        nears.extend(batch)
        parts.append((first, batch))

    last_chunk = len(chunks) - 1
    ready = 2
    passed = 4
    for first in range(edge, groups - edge, edge):
        need = min(first * n_vec + 2 * W, leaves - W)
        while chunks[ready][0] + chunks[ready][1] < need:
            ready += 1
            if ready == last_chunk:
                both(0, rim_copies, takes, landed)
                split_span(0, 0, W)
                split_span(0, leaves + W, W)
                near_span(0, 0, edge)
                near_span(0, groups - edge, edge)
                whole = near_copy(1, 0, 0, groups)
                whole.start()
                keep = pltpu.make_async_copy(nout.at[vi], near.at[vi], near_send.at[0, 0])
                keep.start()
                for d in range(1, n_leaf):
                    @pl.when(li + d < n_leaf)
                    def _(d=d):
                        pays[n_leaf - d - 1].wait_recv()
                        pays[d - 1].start()

                both(1, rim_copies, takes, landed)
                split_span(1, 0, W)
                split_span(1, leaves + W, W)
                near_part(0)
            take(ready)
        near_part(first)
        if passed <= last_chunk:
            pass_on(passed)
            passed += 1
    near_part(groups - edge)

    for d in range(1, n_leaf):
        @pl.when(li + d >= n_leaf)
        def _(d=d):
            pays[n_leaf - d - 1].wait_recv()

    depth = n_leaf.bit_length() - 1

    def cross_at(c):
        return n_leaf - (n_leaf >> (c - 1))

    lifts = [pay[j] for j in range(n_leaf)]
    at = 0
    starts = {}
    for c in range(1, depth):
        nodes = [
            (lifts[2 * j] + lifts[2 * j + 1]) * root_half for j in range(len(lifts) // 2)
        ]
        nodes = [swap(x) if c == 1 else x for x in nodes]
        starts[c] = at
        for j, x in enumerate(nodes):
            hx[at + j] = x
        at += len(nodes)
        if c < depth - 1:
            lifts = []
            for j, x in enumerate(nodes):
                y = dot_nn(x[:, :rank], cross_e_ref[cross_at(c) + j])
                lifts.append(jnp.concatenate([y, y], axis=1))
    z = None
    for c in range(depth - 1, 0, -1):
        node = li >> c
        sibling = node + 1 - 2 * lax.rem(node, 2)
        spot = cross_at(c) + node
        a = cross_flags_ref[spot].astype(f32)
        g = dot_nt(a * hx[starts[c] + sibling][:, :rank], cross_c_ref[spot])
        z = g if z is None else g + dot_nt(z, cross_e_ref[spot])
    sibling = li + 1 - 2 * lax.rem(li, 2)
    a = flags_ref[0, 2 * (last + 1)].astype(f32)
    x = jnp.where(low, a * pay[sibling], jnp.concatenate([z, z], axis=1))
    z = dot_nt(x, top)
    z = jnp.concatenate([z, z], axis=1)

    def down(q, parent):
        h = hp[q]
        a0 = flags_ref[0, 2 * q].astype(f32)
        a1 = flags_ref[0, 2 * q + 1].astype(f32)
        x0 = jnp.where(low, a0 * swap(h), parent)
        x1 = jnp.where(low, a1 * h, parent)
        r = dot_nt(jnp.concatenate([x0, x1], axis=0), mat_pair(q))
        zp[q] = jnp.where(low, r[:8], r[8:])

    down(last, z)
    for (a, count), (b, half) in list(zip(offs[:-1], offs[1:]))[::-1]:
        for t in range(half):
            p = zp[b + t]
            down(a + 2 * t, swap(p))
            down(a + 2 * t + 1, p)

    def far_body(i, carry):
        for w in range(8):
            t = i * 8 + w
            p = zp[t]
            s = swap(p)
            zero = jnp.zeros_like(p)
            for u in range(2):
                pair = 2 * t + u
                first, second = (p, s) if u == 0 else (s, p)
                x = jnp.concatenate(
                    [jnp.where(low, first, zero), jnp.where(low, zero, second)], axis=0
                )
                wt = basis[pl.ds(pl.multiple_of(pair * 128, 128), 128), :]
                r = dot_nn(x, wt)
                far[2 * pair] = r[:8]
                far[2 * pair + 1] = r[8:]
        return carry

    lax.fori_loop(0, leaves // 32, far_body, 0)
    keep.wait()
    whole.wait_recv()

    block = lax.broadcasted_iota(jnp.int32, (8, size), 1) // piece

    def group(g):
        parts = [near[v, g] for v in range(n_vec)]
        for u in range(n_vec):
            leaf = g * n_vec + u
            total = parts[0] if u == 0 else pltpu.roll(parts[0], (size - u * piece), 1)
            for v in range(1, n_vec):
                shift = ((v - u) * piece) % size
                moved = parts[v] if shift == 0 else pltpu.roll(parts[v], shift, 1)
                total = jnp.where(block == v, moved, total)
            spots = inverse[leaf].astype(jnp.int32)
            out_ref[:, pl.ds(pl.multiple_of(leaf * size, size), size)] = jnp.take_along_axis(
                total + far[leaf], spots, axis=1
            )

    for first, batch in parts:
        for c in batch:
            c.wait_recv()
        for g in range(first, first + edge):
            group(g)

    for c in nears + pays + gathers + spreads + [own_copy, whole]:
        c.wait_send()
    for kind in range(2):
        both(kind, halos, sends, lambda c: c.wait_send())
        both(kind, rim_copies, takes, lambda c: c.wait_send())


def local(
    panels,
    near_tiles,
    near_cols,
    leaf_order,
    leaf_basis,
    local_mats,
    local_flags,
    cross_coupling,
    cross_transfer,
    cross_flags,
):
    rows = panels.shape[0]
    leaves, rank, size = leaf_basis.shape
    n_leaf = lax.axis_size("leaf")
    n_vec = lax.axis_size("vec")
    piece = near_tiles.shape[2]
    slots = near_tiles.shape[1]
    vmem = pl.BlockSpec(memory_space=pltpu.VMEM)
    hbm = pl.BlockSpec(memory_space=pl.ANY)
    basis2 = leaf_basis.reshape(leaves * rank, size)
    mats2 = local_mats.reshape(local_mats.shape[1] * rank, 2 * rank)
    groups = leaves // n_vec
    dma = pltpu.SemaphoreType.DMA
    return pl.pallas_call(
        functools.partial(main_kernel, n_leaf, n_vec),
        out_shape=pltpu.VMEM(panels.shape, f32),
        in_specs=[hbm] * 10,
        out_specs=vmem,
        scratch_shapes=[
            pltpu.VMEM(panels.shape, f32),
            pltpu.VMEM(leaf_order.shape, jnp.int32),
            pltpu.SMEM(near_cols.shape[::-1], jnp.int32),
            pltpu.SMEM(local_flags.shape, jnp.int32),
            pltpu.SMEM(cross_flags.shape, jnp.int32),
            pltpu.VMEM(cross_coupling.shape, f32),
            pltpu.VMEM(cross_transfer.shape, f32),
            pltpu.VMEM(near_tiles.shape, f32),
            pltpu.VMEM(basis2.shape, f32),
            pltpu.VMEM(mats2.shape, f32),
            pltpu.VMEM((n_vec, leaves + 2 * W, rows, size), f32),
            pltpu.VMEM((2, leaves + 2 * W, n_vec * rows, size), bf16),
            pltpu.VMEM((leaves, 2 * piece, slots * size), bf16),
            pltpu.VMEM((leaves // 2, rows, size), f32),
            pltpu.VMEM((leaves // 2, rows, size), f32),
            pltpu.VMEM((n_leaf, rows, 2 * rank), f32),
            pltpu.VMEM((n_leaf, rows, 2 * rank), f32),
            pltpu.VMEM((n_vec, groups, rows, size), f32),
            pltpu.VMEM((n_vec, groups, rows, size), f32),
            pltpu.VMEM((leaves, rows, size), f32),
            pltpu.VMEM((leaves, rows, size), f32),
            dma((10,)),
            dma,
            dma,
            dma((6,)),
            dma((6,)),
            dma((6,)),
            dma((6,)),
            dma((2, 2)),
            dma((2, 2)),
            dma((2, 2)),
            dma((2, 2)),
            dma((n_leaf,)),
            dma((n_leaf,)),
            dma((n_vec, groups)),
            dma((n_vec, groups)),
        ],
        compiler_params=pltpu.CompilerParams(
            collective_id=0, has_side_effects=True, vmem_limit_bytes=62 * 1024 * 1024
        ),
        name="tree",
    )(
        panels,
        leaf_order,
        near_cols.T,
        local_flags,
        cross_flags,
        cross_coupling,
        cross_transfer,
        near_tiles,
        basis2,
        mats2,
    )


def solution(mesh):
    return jax.shard_map(
        local,
        mesh=mesh,
        in_specs=(
            P("vec", "leaf"),
            P("leaf", None, "vec", None),
            P("leaf", None),
            P("leaf", None),
            P("leaf", None, None),
            P("leaf", None, None, None),
            P("leaf", None),
            P(),
            P(),
            P(),
        ),
        out_specs=P("vec", "leaf"),
        check_vma=False,
    )
```

```python
import functools
import math

import jax
import jax.numpy as jnp
from jax import lax
from jax.experimental import pallas as pl
from jax.experimental.pallas import tpu as pltpu
from jax.sharding import PartitionSpec as P

W = 8
f32 = jnp.float32
bf16 = jnp.bfloat16
root_half = 1.0 / math.sqrt(2.0)
MESH = pl.DeviceIdType.MESH
NN = (((1,), (0,)), ((), ()))
NT = (((1,), (1,)), ((), ()))


def halves(x):
    high = x.astype(bf16).astype(f32)
    return high, x - high


def stacked(x):
    return jnp.concatenate(halves(x), axis=0).astype(bf16)


def split(w):
    high = w.astype(bf16)
    return high, (w - high.astype(f32)).astype(bf16)


def dot_nt(x, w):
    rows = x.shape[0]
    lhs = stacked(x)
    r = lax.dot_general(
        jnp.concatenate([lhs, lhs], axis=1),
        jnp.concatenate(split(w), axis=1),
        NT,
        preferred_element_type=f32,
    )
    return r[:rows] + r[rows:]


def dot_nn(x, w):
    rows, cols = x.shape[0], w.shape[1]
    r = lax.dot_general(
        stacked(x), jnp.concatenate(split(w), axis=1), NN, preferred_element_type=f32
    )
    r = r[:, :cols] + r[:, cols:]
    return r[:rows] + r[rows:]


def hot_of(order_row):
    size = order_row.shape[1]
    rows = lax.broadcasted_iota(jnp.int32, (size, size), 0)
    return jnp.where(rows == order_row, 1.0, 0.0).astype(bf16)


def main_kernel(
    n_leaf,
    n_vec,
    panels_hbm,
    order_hbm,
    cols_hbm,
    flags_hbm,
    cross_flags_hbm,
    cross_c_hbm,
    cross_e_hbm,
    tiles_hbm,
    basis_hbm,
    mats_hbm,
    out_ref,
    panels,
    order,
    cols_ref,
    flags_ref,
    cross_flags_ref,
    cross_c_ref,
    cross_e_ref,
    tiles,
    basis,
    mats,
    ext,
    xs,
    tb,
    hp,
    zp,
    pay,
    hx,
    nout,
    near,
    far,
    inverse,
    load_sem,
    own_send,
    own_recv,
    gather_send,
    gather_recv,
    spread_send,
    spread_recv,
    halo_send,
    halo_recv,
    rim_send,
    rim_recv,
    pay_send,
    pay_recv,
    near_send,
    near_recv,
    inv_send,
    inv_recv,
):
    leaves, size = order.shape
    rank = 64
    slots = tiles.shape[1]
    piece = tiles.shape[2]
    groups = leaves // n_vec
    li = lax.axis_index("leaf")
    vi = lax.axis_index("vec")
    loads = [
        pltpu.make_async_copy(src, dst, load_sem.at[i])
        for i, (src, dst) in enumerate(
            [
                (panels_hbm, panels),
                (order_hbm, order),
                (basis_hbm, basis),
                (mats_hbm, mats),
                (tiles_hbm, tiles),
                (cols_hbm, cols_ref),
                (flags_hbm, flags_ref),
                (cross_flags_hbm, cross_flags_ref),
                (cross_c_hbm, cross_c_ref),
                (cross_e_hbm, cross_e_ref),
            ]
        )
    ]
    load_p, load_o, load_b, load_m, load_t = loads[:5]
    small = loads[5:]
    for c in loads[:3]:
        c.start()

    barrier = pltpu.get_barrier_semaphore()
    for d in range(1, n_vec):
        pl.semaphore_signal(
            barrier, inc=1, device_id=(li, lax.rem(vi + d, n_vec)), device_id_type=MESH
        )
    for d in range(1, n_leaf):
        @pl.when(li + d < n_leaf)
        def _(d=d):
            pl.semaphore_signal(
                barrier, inc=1, device_id=(lax.rem(li + d, n_leaf), vi), device_id_type=MESH
            )
    load_m.start()
    for c in small:
        c.start()

    assert n_vec == 4
    beside = vi + 1 - 2 * lax.rem(vi, 2)
    across = lax.rem(vi + 2, n_vec)
    here = vi - lax.rem(vi, 2)
    there = lax.rem(here + 2, n_vec)
    has_left = li > 0
    has_right = li < n_leaf - 1
    chunks = [(0, W), (leaves - W, W)]
    at = W
    while at < leaves - W:
        wide = 2 * W if leaves - W - at > 2 * W else W
        chunks.append((at, wide))
        at += wide

    own_copy = pltpu.make_async_remote_copy(
        src_ref=ext.at[vi, pl.ds(W, leaves)],
        dst_ref=ext.at[vi, pl.ds(W, leaves)],
        send_sem=own_send,
        recv_sem=own_recv,
        device_id=(li, beside),
        device_id_type=MESH,
    )

    def gather_copy(k, target):
        sems = (gather_send, gather_recv) if target is across else (spread_send, spread_recv)
        block = ext.at[vi, pl.ds(W + chunks[k][0], chunks[k][1])]
        return pltpu.make_async_remote_copy(
            src_ref=block,
            dst_ref=block,
            send_sem=sems[0].at[k],
            recv_sem=sems[1].at[k],
            device_id=(li, target),
            device_id_type=MESH,
        )

    def spread_copy(k):
        block = ext.at[across, pl.ds(W + chunks[k][0], chunks[k][1])]
        return pltpu.make_async_remote_copy(
            src_ref=block,
            dst_ref=block,
            send_sem=spread_send.at[k],
            recv_sem=spread_recv.at[k],
            device_id=(li, beside),
            device_id_type=MESH,
        )

    rims = (0, leaves + W)
    sends = (has_right, has_left)
    takes = (has_left, has_right)

    def halo_copy(side, kind):
        vec = vi if kind == 0 else across
        target = jnp.minimum(li + 1, n_leaf - 1) if side == 0 else jnp.maximum(li - 1, 0)
        return pltpu.make_async_remote_copy(
            src_ref=ext.at[vec, pl.ds(leaves if side == 0 else W, W)],
            dst_ref=ext.at[vec, pl.ds(rims[side], W)],
            send_sem=halo_send.at[side, kind],
            recv_sem=halo_recv.at[side, kind],
            device_id=(target, vi),
            device_id_type=MESH,
        )

    def rim_copy(side, kind):
        block = ext.at[vi if kind == 0 else across, pl.ds(rims[side], W)]
        return pltpu.make_async_remote_copy(
            src_ref=block,
            dst_ref=block,
            send_sem=rim_send.at[side, kind],
            recv_sem=rim_recv.at[side, kind],
            device_id=(li, beside),
            device_id_type=MESH,
        )

    last_chunk = len(chunks) - 1
    gathers = [gather_copy(k, across) for k in range(len(chunks))]
    spreads = [spread_copy(k) for k in range(last_chunk)]
    spreads.append(gather_copy(last_chunk, n_vec - 1 - vi))
    halos = [[halo_copy(side, kind) for side in range(2)] for kind in range(2)]
    rim_copies = [[rim_copy(side, kind) for side in range(2)] for kind in range(2)]

    def begin(c):
        c.start()

    def landed(c):
        c.wait_recv()

    def one(side, kind, copies, conditions, act):
        @pl.when(conditions[side])
        def _():
            act(copies[kind][side])

    def both(kind, copies, conditions, act):
        for side in range(2):
            one(side, kind, copies, conditions, act)

    lane = lax.broadcasted_iota(jnp.int32, (8, 2 * rank), 1)
    low = lane < rank

    def swap(x):
        return pltpu.roll(x, rank, 1)

    load_p.wait()
    load_o.wait()

    def order_body(i, carry):
        for u in range(32):
            leaf = i * 32 + u
            x = panels[:, pl.ds(pl.multiple_of(leaf * size, size), size)]
            spots = jnp.broadcast_to(order[pl.ds(leaf, 1), :], x.shape)
            ext[vi, W + leaf] = jnp.take_along_axis(x, spots, axis=1)
        return carry

    lax.fori_loop(0, leaves // 32, order_body, 0)
    pl.semaphore_wait(barrier, n_vec - 1 + li)
    for c in gathers + spreads[last_chunk:]:
        c.start()
    own_copy.start()
    one(1, 0, halos, sends, begin)
    load_b.wait()
    load_t.start()

    def skel_body(i, carry):
        for w in range(8):
            t = i * 8 + w
            sums = []
            for u in range(2):
                pair = t * 2 + u
                x = ext[vi, pl.ds(W + pair * 2, 2)].reshape(16, 128)
                wt = basis[pl.ds(pl.multiple_of(pair * 128, 128), 128), :]
                r = dot_nt(x, wt)
                sums.append((r[:8], r[8:]))
            even = sums[0][0] + swap(sums[0][1])
            odd = swap(sums[1][0]) + sums[1][1]
            hp[t] = jnp.where(low, even, odd) * root_half
        return carry

    lax.fori_loop(0, leaves // 32, skel_body, 0)
    load_m.wait()

    def mat_pair(q):
        return mats[pl.ds(pl.multiple_of(q * 128, 128), 128), :]

    def up(off, nxt, t):
        r0 = dot_nn(hp[off + 2 * t], mat_pair(off + 2 * t))
        r1 = dot_nn(hp[off + 2 * t + 1], mat_pair(off + 2 * t + 1))
        hp[nxt + t] = jnp.where(low, swap(r0), r1) * root_half

    pairs = leaves // 4
    offs = []
    off = 0
    while pairs >= 1:
        offs.append((off, pairs))
        off += pairs
        pairs //= 2
    for (a, count), (b, half) in zip(offs[:-1], offs[1:]):
        for t in range(half):
            up(a, b, t)
    last = offs[-1][0]
    r = dot_nn(hp[last], mat_pair(last))
    skel = swap(r) * root_half
    top = mats[pl.ds((last + 1) * 128, rank), :]
    lift = dot_nn(skel[:, :rank], top)
    pay[li] = jnp.where(low, skel, lift)

    def pay_copy(d):
        return pltpu.make_async_remote_copy(
            src_ref=pay.at[li],
            dst_ref=pay.at[li],
            send_sem=pay_send.at[d],
            recv_sem=pay_recv.at[n_leaf - d],
            device_id=(lax.rem(li + d, n_leaf), vi),
            device_id_type=MESH,
        )

    pays = [pay_copy(d) for d in range(1, n_leaf)]

    for d in range(1, n_leaf):
        @pl.when(li + d >= n_leaf)
        def _(d=d):
            pays[d - 1].start()

    counts = lax.broadcasted_iota(jnp.int32, (8, size), 1).astype(f32)
    spot_row = lax.broadcasted_iota(jnp.int32, (8, size), 0)
    share = leaves // n_vec

    def picked(w):
        return jnp.where(spot_row == w, counts, 0.0)

    for first in range(0, share, 8):
        start = vi * share + first
        rows = order[pl.ds(pl.multiple_of(start, 8), 8), :]
        total = None
        for w in range(0, 8, 2):
            lhs = jnp.concatenate([picked(w), picked(w + 1)], axis=1).astype(bf16)
            hot = jnp.concatenate([hot_of(rows[w : w + 1]), hot_of(rows[w + 1 : w + 2])], axis=1)
            r = lax.dot_general(lhs, hot, NT, preferred_element_type=f32)
            total = r if total is None else total + r
        inverse[pl.ds(pl.multiple_of(start, 8), 8), :] = total

    def inverse_copy(d):
        block = inverse.at[pl.ds(pl.multiple_of(vi * share, 8), share)]
        return pltpu.make_async_remote_copy(
            src_ref=block,
            dst_ref=block,
            send_sem=inv_send.at[d],
            recv_sem=inv_recv.at[n_vec - d],
            device_id=(li, lax.rem(vi + d, n_vec)),
            device_id_type=MESH,
        )

    inverses = [inverse_copy(d) for d in range(1, n_vec)]
    for c in inverses:
        c.start()

    def split_span(side, first, count):
        block = here if side == 0 else there

        def body(i, carry):
            for w in range(8):
                e = first + i * 8 + w
                x = ext[pl.ds(block, 2), e].reshape(16, 128)
                xs[side, e] = stacked(x)
            return carry

        lax.fori_loop(0, count // 8, body, 0)

    for c in small:
        c.wait()
    own_copy.wait_recv()
    split_span(0, W, leaves)
    load_t.wait()
    base = li * leaves - W

    def place(leaf, n):
        return jnp.clip(cols_ref[n, leaf] - base, 0, leaves + 2 * W - 1)

    def near_group(side, g):
        outs = []
        for w in range(n_vec):
            leaf = g * n_vec + w
            x = jnp.concatenate([xs[side, place(leaf, n)] for n in range(slots)], axis=1)
            if side == 0:
                t = jnp.concatenate([stacked(tiles[leaf, n]) for n in range(slots)], axis=1)
                tb[leaf] = t
            else:
                t = tb[leaf]
            r = lax.dot_general(x, t, NT, preferred_element_type=f32)
            r = r[:16] + r[16:]
            outs.append(r[:, :piece] + r[:, piece:])
        block = here if side == 0 else there
        nout[pl.ds(block, 2), g] = jnp.concatenate(outs, axis=1).reshape(2, 8, n_vec * piece)

    def near_span(side, first, count):
        def body(i, carry):
            for w in range(4):
                near_group(side, first + i * 4 + w)
            return carry

        lax.fori_loop(0, count // 4, body, 0)
        for g in range(first + count // 4 * 4, first + count):
            near_group(side, g)

    edge = W // n_vec
    middle = groups - 2 * edge

    def pass_on(k):
        gathers[k].wait_recv()
        spreads[k].start()

    def take(k):
        spreads[k].wait_recv()
        split_span(1, W + chunks[k][0], chunks[k][1])

    near_span(0, edge, middle // 2)
    pass_on(0)
    pass_on(1)
    one(1, 0, halos, takes, landed)
    one(0, 0, halos, sends, begin)
    both(1, halos, sends, begin)
    one(1, 0, rim_copies, takes, begin)
    def near_copy(d, part, first, count):
        u = across if d == 2 else (beside if d == 1 else n_vec - 1 - vi)
        span = pl.ds(first, count)
        return pltpu.make_async_remote_copy(
            src_ref=nout.at[u, span],
            dst_ref=near.at[vi, span],
            send_sem=near_send.at[0 if d == 1 else 2 * part + d],
            recv_sem=near_recv.at[0 if d == 1 else 2 * part + d],
            device_id=(li, u),
            device_id_type=MESH,
        )

    nears = []
    parts = []

    def near_part(first):
        near_span(1, first, edge)
        batch = [near_copy(d, len(parts), first, edge) for d in (2, 3)]
        for c in batch:
            c.start()
        nears.extend(batch)
        parts.append((first, batch))

    pass_on(2)
    near_span(0, edge + middle // 2, middle - middle // 2)
    one(0, 0, halos, takes, landed)
    one(0, 0, rim_copies, takes, begin)
    take(0)
    take(1)
    pass_on(3)
    both(0, rim_copies, takes, landed)
    split_span(0, 0, W)
    split_span(0, leaves + W, W)
    near_span(0, 0, edge)
    near_span(0, groups - edge, edge)
    whole = near_copy(1, 0, 0, groups)
    whole.start()
    keep = pltpu.make_async_copy(nout.at[vi], near.at[vi], near_send.at[1])
    keep.start()
    take(2)
    near_part(edge)
    both(1, halos, takes, landed)
    both(1, rim_copies, takes, begin)
    ready = 2
    for first in range(2 * edge, groups - edge, edge):
        need = min(first * n_vec + 2 * W, leaves - W)
        while chunks[ready][0] + chunks[ready][1] < need:
            ready += 1
            if ready == last_chunk:
                both(1, rim_copies, takes, landed)
                split_span(1, 0, W)
                split_span(1, leaves + W, W)
                near_part(0)
            elif ready + 1 < last_chunk:
                pass_on(ready + 1)
            else:
                gathers[last_chunk].wait_recv()
                for d in range(1, n_leaf):
                    @pl.when(li + d < n_leaf)
                    def _(d=d):
                        pays[n_leaf - d - 1].wait_recv()
                        pays[d - 1].start()

            take(ready)
        near_part(first)
    near_part(groups - edge)

    for d in range(1, n_leaf):
        @pl.when(li + d >= n_leaf)
        def _(d=d):
            pays[n_leaf - d - 1].wait_recv()

    depth = n_leaf.bit_length() - 1

    def cross_at(c):
        return n_leaf - (n_leaf >> (c - 1))

    lifts = [pay[j] for j in range(n_leaf)]
    at = 0
    starts = {}
    for c in range(1, depth):
        nodes = [
            (lifts[2 * j] + lifts[2 * j + 1]) * root_half for j in range(len(lifts) // 2)
        ]
        nodes = [swap(x) if c == 1 else x for x in nodes]
        starts[c] = at
        for j, x in enumerate(nodes):
            hx[at + j] = x
        at += len(nodes)
        if c < depth - 1:
            lifts = []
            for j, x in enumerate(nodes):
                y = dot_nn(x[:, :rank], cross_e_ref[cross_at(c) + j])
                lifts.append(jnp.concatenate([y, y], axis=1))
    z = None
    for c in range(depth - 1, 0, -1):
        node = li >> c
        sibling = node + 1 - 2 * lax.rem(node, 2)
        spot = cross_at(c) + node
        a = cross_flags_ref[spot].astype(f32)
        g = dot_nt(a * hx[starts[c] + sibling][:, :rank], cross_c_ref[spot])
        z = g if z is None else g + dot_nt(z, cross_e_ref[spot])
    sibling = li + 1 - 2 * lax.rem(li, 2)
    a = flags_ref[0, 2 * (last + 1)].astype(f32)
    x = jnp.where(low, a * pay[sibling], jnp.concatenate([z, z], axis=1))
    z = dot_nt(x, top)
    z = jnp.concatenate([z, z], axis=1)

    def down(q, parent):
        h = hp[q]
        a0 = flags_ref[0, 2 * q].astype(f32)
        a1 = flags_ref[0, 2 * q + 1].astype(f32)
        x0 = jnp.where(low, a0 * swap(h), parent)
        x1 = jnp.where(low, a1 * h, parent)
        r = dot_nt(jnp.concatenate([x0, x1], axis=0), mat_pair(q))
        zp[q] = jnp.where(low, r[:8], r[8:])

    down(last, z)
    for (a, count), (b, half) in list(zip(offs[:-1], offs[1:]))[::-1]:
        for t in range(half):
            p = zp[b + t]
            down(a + 2 * t, swap(p))
            down(a + 2 * t + 1, p)

    def far_body(i, carry):
        for w in range(8):
            t = i * 8 + w
            p = zp[t]
            s = swap(p)
            zero = jnp.zeros_like(p)
            for u in range(2):
                pair = 2 * t + u
                first, second = (p, s) if u == 0 else (s, p)
                x = jnp.concatenate(
                    [jnp.where(low, first, zero), jnp.where(low, zero, second)], axis=0
                )
                wt = basis[pl.ds(pl.multiple_of(pair * 128, 128), 128), :]
                r = dot_nn(x, wt)
                far[2 * pair] = r[:8]
                far[2 * pair + 1] = r[8:]
        return carry

    lax.fori_loop(0, leaves // 32, far_body, 0)
    keep.wait()
    whole.wait_recv()

    for c in inverses:
        c.wait_recv()
    lanes = lax.broadcasted_iota(jnp.int32, (8, size), 1)
    left = lanes < 2 * piece
    even = lax.rem(lanes // piece, 2) == 0

    def halves_of(x, y):
        moved = pltpu.roll(jnp.where(left, y, x), 2 * piece, 1)
        return jnp.where(left, x, moved), jnp.where(left, moved, y)

    def quarters_of(x, y):
        mixed = jnp.where(even, y, x)
        return (
            jnp.where(even, x, pltpu.roll(mixed, piece, 1)),
            jnp.where(even, pltpu.roll(mixed, size - piece, 1), y),
        )

    def group(g):
        p0, p1, p2, p3 = [near[v, g] for v in range(n_vec)]
        a0, a2 = halves_of(p0, p2)
        a1, a3 = halves_of(p1, p3)
        rows = quarters_of(a0, a1) + quarters_of(a2, a3)
        for u in range(n_vec):
            leaf = g * n_vec + u
            spots = jnp.broadcast_to(inverse[pl.ds(leaf, 1), :], (8, size)).astype(jnp.int32)
            out_ref[:, pl.ds(pl.multiple_of(leaf * size, size), size)] = jnp.take_along_axis(
                rows[u] + far[leaf], spots, axis=1
            )

    for batch in (parts[: len(parts) - 3], parts[len(parts) - 3 :]):
        for _, copies in batch:
            for c in copies:
                c.wait_recv()
        for first, _ in batch:
            for g in range(first, first + edge):
                group(g)

    for c in nears + pays + gathers + spreads + inverses + [own_copy, whole]:
        c.wait_send()
    for kind in range(2):
        both(kind, halos, sends, lambda c: c.wait_send())
        both(kind, rim_copies, takes, lambda c: c.wait_send())


def local(
    panels,
    near_tiles,
    near_cols,
    leaf_order,
    leaf_basis,
    local_mats,
    local_flags,
    cross_coupling,
    cross_transfer,
    cross_flags,
):
    rows = panels.shape[0]
    leaves, rank, size = leaf_basis.shape
    n_leaf = lax.axis_size("leaf")
    n_vec = lax.axis_size("vec")
    piece = near_tiles.shape[2]
    slots = near_tiles.shape[1]
    vmem = pl.BlockSpec(memory_space=pltpu.VMEM)
    hbm = pl.BlockSpec(memory_space=pl.ANY)
    basis2 = leaf_basis.reshape(leaves * rank, size)
    mats2 = local_mats.reshape(local_mats.shape[1] * rank, 2 * rank)
    groups = leaves // n_vec
    dma = pltpu.SemaphoreType.DMA
    return pl.pallas_call(
        functools.partial(main_kernel, n_leaf, n_vec),
        out_shape=pltpu.VMEM(panels.shape, f32),
        in_specs=[hbm] * 10,
        out_specs=vmem,
        scratch_shapes=[
            pltpu.VMEM(panels.shape, f32),
            pltpu.VMEM(leaf_order.shape, jnp.int32),
            pltpu.SMEM(near_cols.shape[::-1], jnp.int32),
            pltpu.SMEM(local_flags.shape, jnp.int32),
            pltpu.SMEM(cross_flags.shape, jnp.int32),
            pltpu.VMEM(cross_coupling.shape, f32),
            pltpu.VMEM(cross_transfer.shape, f32),
            pltpu.VMEM(near_tiles.shape, f32),
            pltpu.VMEM(basis2.shape, f32),
            pltpu.VMEM(mats2.shape, f32),
            pltpu.VMEM((n_vec, leaves + 2 * W, rows, size), f32),
            pltpu.VMEM((2, leaves + 2 * W, n_vec * rows, size), bf16),
            pltpu.VMEM((leaves, 2 * piece, slots * size), bf16),
            pltpu.VMEM((leaves // 2, rows, size), f32),
            pltpu.VMEM((leaves // 2, rows, size), f32),
            pltpu.VMEM((n_leaf, rows, 2 * rank), f32),
            pltpu.VMEM((n_leaf, rows, 2 * rank), f32),
            pltpu.VMEM((n_vec, groups, rows, size), f32),
            pltpu.VMEM((n_vec, groups, rows, size), f32),
            pltpu.VMEM((leaves, rows, size), f32),
            pltpu.VMEM((leaves, size), f32),
            dma((10,)),
            dma,
            dma,
            dma((6,)),
            dma((6,)),
            dma((6,)),
            dma((6,)),
            dma((2, 2)),
            dma((2, 2)),
            dma((2, 2)),
            dma((2, 2)),
            dma((n_leaf,)),
            dma((n_leaf,)),
            dma((2 + leaves // W * 2,)),
            dma((2 + leaves // W * 2,)),
            dma((n_vec,)),
            dma((n_vec,)),
        ],
        compiler_params=pltpu.CompilerParams(
            collective_id=0, has_side_effects=True, vmem_limit_bytes=62 * 1024 * 1024
        ),
        name="tree",
    )(
        panels,
        leaf_order,
        near_cols.T,
        local_flags,
        cross_flags,
        cross_coupling,
        cross_transfer,
        near_tiles,
        basis2,
        mats2,
    )


def solution(mesh):
    return jax.shard_map(
        local,
        mesh=mesh,
        in_specs=(
            P("vec", "leaf"),
            P("leaf", None, "vec", None),
            P("leaf", None),
            P("leaf", None),
            P("leaf", None, None),
            P("leaf", None, None, None),
            P("leaf", None),
            P(),
            P(),
            P(),
        ),
        out_specs=P("vec", "leaf"),
        check_vma=False,
    )
```

```python
import functools
import math

import jax
import jax.numpy as jnp
from jax import lax
from jax.experimental import pallas as pl
from jax.experimental.pallas import tpu as pltpu
from jax.sharding import PartitionSpec as P

W = 8
f32 = jnp.float32
bf16 = jnp.bfloat16
root_half = 1.0 / math.sqrt(2.0)
MESH = pl.DeviceIdType.MESH
NN = (((1,), (0,)), ((), ()))
NT = (((1,), (1,)), ((), ()))


def halves(x):
    high = x.astype(bf16).astype(f32)
    return high, x - high


def stacked(x):
    return jnp.concatenate(halves(x), axis=0).astype(bf16)


def split(w):
    high = w.astype(bf16)
    return high, (w - high.astype(f32)).astype(bf16)


def dot_nt(x, w):
    rows = x.shape[0]
    lhs = stacked(x)
    r = lax.dot_general(
        jnp.concatenate([lhs, lhs], axis=1),
        jnp.concatenate(split(w), axis=1),
        NT,
        preferred_element_type=f32,
    )
    return r[:rows] + r[rows:]


def dot_nn(x, w):
    rows, cols = x.shape[0], w.shape[1]
    r = lax.dot_general(
        stacked(x), jnp.concatenate(split(w), axis=1), NN, preferred_element_type=f32
    )
    r = r[:, :cols] + r[:, cols:]
    return r[:rows] + r[rows:]


def hot_of(order_row):
    size = order_row.shape[1]
    rows = lax.broadcasted_iota(jnp.int32, (size, size), 0)
    return jnp.where(rows == order_row, 1.0, 0.0).astype(bf16)


def main_kernel(
    n_leaf,
    n_vec,
    panels_hbm,
    order_hbm,
    cols_hbm,
    flags_hbm,
    cross_flags_hbm,
    cross_c_hbm,
    cross_e_hbm,
    tiles_hbm,
    basis_hbm,
    mats_hbm,
    out_ref,
    panels,
    order,
    cols_ref,
    flags_ref,
    cross_flags_ref,
    cross_c_ref,
    cross_e_ref,
    tiles,
    basis,
    mats,
    ext,
    xs,
    tb,
    hp,
    zp,
    pay,
    hx,
    nout,
    near,
    far,
    inverse,
    load_sem,
    own_send,
    own_recv,
    gather_send,
    gather_recv,
    spread_send,
    spread_recv,
    halo_send,
    halo_recv,
    rim_send,
    rim_recv,
    pay_send,
    pay_recv,
    near_send,
    near_recv,
    inv_send,
    inv_recv,
    hello,
):
    leaves, size = order.shape
    rank = 64
    slots = tiles.shape[1]
    piece = tiles.shape[2]
    groups = leaves // n_vec
    li = lax.axis_index("leaf")
    vi = lax.axis_index("vec")
    loads = [
        pltpu.make_async_copy(src, dst, load_sem.at[i])
        for i, (src, dst) in enumerate(
            [
                (panels_hbm, panels),
                (order_hbm, order),
                (basis_hbm, basis),
                (mats_hbm, mats),
                (tiles_hbm, tiles),
                (cols_hbm, cols_ref),
                (flags_hbm, flags_ref),
                (cross_flags_hbm, cross_flags_ref),
                (cross_c_hbm, cross_c_ref),
                (cross_e_hbm, cross_e_ref),
            ]
        )
    ]
    load_p, load_o, load_b, load_m, load_t = loads[:5]
    small = loads[5:]
    for c in loads[:3]:
        c.start()

    barrier = pltpu.get_barrier_semaphore()
    for d in range(1, n_vec):
        pl.semaphore_signal(
            barrier, inc=1, device_id=(li, lax.rem(vi + d, n_vec)), device_id_type=MESH
        )
    for d in range(1, n_leaf):
        @pl.when(li + d < n_leaf)
        def _(d=d):
            pl.semaphore_signal(
                barrier, inc=1, device_id=(lax.rem(li + d, n_leaf), vi), device_id_type=MESH
            )
    load_m.start()
    for c in small:
        c.start()

    assert n_vec == 4
    beside = vi + 1 - 2 * lax.rem(vi, 2)
    across = lax.rem(vi + 2, n_vec)
    here = vi - lax.rem(vi, 2)
    there = lax.rem(here + 2, n_vec)
    has_left = li > 0
    has_right = li < n_leaf - 1
    chunks = [(0, W), (leaves - W, W)]
    at = W
    while at < leaves - W:
        wide = 2 * W if leaves - W - at > 2 * W else W
        chunks.append((at, wide))
        at += wide

    own_copy = pltpu.make_async_remote_copy(
        src_ref=ext.at[vi, pl.ds(W, leaves)],
        dst_ref=ext.at[vi, pl.ds(W, leaves)],
        send_sem=own_send,
        recv_sem=own_recv,
        device_id=(li, beside),
        device_id_type=MESH,
    )

    def gather_copy(k, target):
        sems = (gather_send, gather_recv) if target is across else (spread_send, spread_recv)
        block = ext.at[vi, pl.ds(W + chunks[k][0], chunks[k][1])]
        return pltpu.make_async_remote_copy(
            src_ref=block,
            dst_ref=block,
            send_sem=sems[0].at[k],
            recv_sem=sems[1].at[k],
            device_id=(li, target),
            device_id_type=MESH,
        )

    def spread_copy(k):
        block = ext.at[across, pl.ds(W + chunks[k][0], chunks[k][1])]
        return pltpu.make_async_remote_copy(
            src_ref=block,
            dst_ref=block,
            send_sem=spread_send.at[k],
            recv_sem=spread_recv.at[k],
            device_id=(li, beside),
            device_id_type=MESH,
        )

    rims = (0, leaves + W)
    sends = (has_right, has_left)
    takes = (has_left, has_right)

    def halo_copy(side, kind):
        vec = vi if kind == 0 else across
        target = jnp.minimum(li + 1, n_leaf - 1) if side == 0 else jnp.maximum(li - 1, 0)
        return pltpu.make_async_remote_copy(
            src_ref=ext.at[vec, pl.ds(leaves if side == 0 else W, W)],
            dst_ref=ext.at[vec, pl.ds(rims[side], W)],
            send_sem=halo_send.at[side, kind],
            recv_sem=halo_recv.at[side, kind],
            device_id=(target, vi),
            device_id_type=MESH,
        )

    def rim_copy(side, kind):
        block = ext.at[vi if kind == 0 else across, pl.ds(rims[side], W)]
        return pltpu.make_async_remote_copy(
            src_ref=block,
            dst_ref=block,
            send_sem=rim_send.at[side, kind],
            recv_sem=rim_recv.at[side, kind],
            device_id=(li, beside),
            device_id_type=MESH,
        )

    last_chunk = len(chunks) - 1
    gathers = [gather_copy(k, across) for k in range(len(chunks))]
    spreads = [spread_copy(k) for k in range(last_chunk)]
    spreads.append(gather_copy(last_chunk, n_vec - 1 - vi))
    halos = [[halo_copy(side, kind) for side in range(2)] for kind in range(2)]
    rim_copies = [[rim_copy(side, kind) for side in range(2)] for kind in range(2)]

    def begin(c):
        c.start()

    def landed(c):
        c.wait_recv()

    def one(side, kind, copies, conditions, act):
        @pl.when(conditions[side])
        def _():
            act(copies[kind][side])

    def both(kind, copies, conditions, act):
        for side in range(2):
            one(side, kind, copies, conditions, act)

    lane = lax.broadcasted_iota(jnp.int32, (8, 2 * rank), 1)
    low = lane < rank

    def swap(x):
        return pltpu.roll(x, rank, 1)

    load_p.wait()
    load_o.wait()

    def order_span(first, count):
        for leaf in range(first, first + count):
            x = panels[:, leaf * size : (leaf + 1) * size]
            spots = jnp.broadcast_to(order[pl.ds(leaf, 1), :], x.shape)
            ext[vi, W + leaf] = jnp.take_along_axis(x, spots, axis=1)

    early = (li == 0) & (here == 0)

    def greet_lower():
        own_copy.start()
        spreads[last_chunk].start()
        for d in range(1, n_leaf):
            @pl.when(li + d >= n_leaf)
            def _(d=d):
                pl.semaphore_signal(
                    hello, inc=1, device_id=(lax.rem(li + d, n_leaf), vi), device_id_type=MESH
                )

    @pl.when(jnp.logical_not(early))
    def _():
        order_span(*chunks[0])
        order_span(*chunks[1])
        pl.semaphore_wait(barrier, n_vec - 1 + li)
        gathers[0].start()
        gathers[1].start()
        one(1, 0, halos, sends, begin)
        for k in range(2, len(chunks)):
            order_span(*chunks[k])
            gathers[k].start()
        greet_lower()

    @pl.when(early)
    def _():
        for k in range(len(chunks)):
            order_span(*chunks[k])

    load_b.wait()
    load_t.start()

    def skel_body(i, carry):
        for w in range(8):
            t = i * 8 + w
            sums = []
            for u in range(2):
                pair = t * 2 + u
                x = ext[vi, pl.ds(W + pair * 2, 2)].reshape(16, 128)
                wt = basis[pl.ds(pl.multiple_of(pair * 128, 128), 128), :]
                r = dot_nt(x, wt)
                sums.append((r[:8], r[8:]))
            even = sums[0][0] + swap(sums[0][1])
            odd = swap(sums[1][0]) + sums[1][1]
            hp[t] = jnp.where(low, even, odd) * root_half
        return carry

    lax.fori_loop(0, leaves // 32, skel_body, 0)

    @pl.when(early)
    def _():
        pl.semaphore_wait(barrier, n_vec - 1 + li)
        for c in gathers:
            c.start()
        one(1, 0, halos, sends, begin)
        greet_lower()

    load_m.wait()

    def mat_pair(q):
        return mats[pl.ds(pl.multiple_of(q * 128, 128), 128), :]

    def up(off, nxt, t):
        r0 = dot_nn(hp[off + 2 * t], mat_pair(off + 2 * t))
        r1 = dot_nn(hp[off + 2 * t + 1], mat_pair(off + 2 * t + 1))
        hp[nxt + t] = jnp.where(low, swap(r0), r1) * root_half

    pairs = leaves // 4
    offs = []
    off = 0
    while pairs >= 1:
        offs.append((off, pairs))
        off += pairs
        pairs //= 2
    for (a, count), (b, half) in zip(offs[:-1], offs[1:]):
        for t in range(half):
            up(a, b, t)
    last = offs[-1][0]
    r = dot_nn(hp[last], mat_pair(last))
    skel = swap(r) * root_half
    top = mats[pl.ds((last + 1) * 128, rank), :]
    lift = dot_nn(skel[:, :rank], top)
    pay[li] = jnp.where(low, skel, lift)

    def pay_copy(d):
        return pltpu.make_async_remote_copy(
            src_ref=pay.at[li],
            dst_ref=pay.at[li],
            send_sem=pay_send.at[d],
            recv_sem=pay_recv.at[n_leaf - d],
            device_id=(lax.rem(li + d, n_leaf), vi),
            device_id_type=MESH,
        )

    pays = [pay_copy(d) for d in range(1, n_leaf)]

    for d in range(1, n_leaf):
        @pl.when(li + d >= n_leaf)
        def _(d=d):
            pays[d - 1].start()

    counts = lax.broadcasted_iota(jnp.int32, (8, size), 1).astype(f32)
    spot_row = lax.broadcasted_iota(jnp.int32, (8, size), 0)
    share = leaves // n_vec

    def picked(w):
        return jnp.where(spot_row == w, counts, 0.0)

    for first in range(0, share, 8):
        start = vi * share + first
        rows = order[pl.ds(pl.multiple_of(start, 8), 8), :]
        total = None
        for w in range(0, 8, 2):
            lhs = jnp.concatenate([picked(w), picked(w + 1)], axis=1).astype(bf16)
            hot = jnp.concatenate([hot_of(rows[w : w + 1]), hot_of(rows[w + 1 : w + 2])], axis=1)
            r = lax.dot_general(lhs, hot, NT, preferred_element_type=f32)
            total = r if total is None else total + r
        inverse[pl.ds(pl.multiple_of(start, 8), 8), :] = total

    def inverse_copy(d):
        block = inverse.at[pl.ds(pl.multiple_of(vi * share, 8), share)]
        return pltpu.make_async_remote_copy(
            src_ref=block,
            dst_ref=block,
            send_sem=inv_send.at[d],
            recv_sem=inv_recv.at[n_vec - d],
            device_id=(li, lax.rem(vi + d, n_vec)),
            device_id_type=MESH,
        )

    inverses = [inverse_copy(d) for d in range(1, n_vec)]
    for c in inverses:
        c.start()

    def split_span(side, first, count):
        block = here if side == 0 else there

        def body(i, carry):
            for w in range(8):
                e = first + i * 8 + w
                x = ext[pl.ds(block, 2), e].reshape(16, 128)
                xs[side, e] = stacked(x)
            return carry

        lax.fori_loop(0, count // 8, body, 0)

    for c in small:
        c.wait()
    own_copy.wait_recv()
    split_span(0, W, leaves)
    load_t.wait()
    base = li * leaves - W

    def place(leaf, n):
        return jnp.clip(cols_ref[n, leaf] - base, 0, leaves + 2 * W - 1)

    def near_group(side, g):
        outs = []
        for w in range(n_vec):
            leaf = g * n_vec + w
            x = jnp.concatenate([xs[side, place(leaf, n)] for n in range(slots)], axis=1)
            if side == 0:
                t = jnp.concatenate([stacked(tiles[leaf, n]) for n in range(slots)], axis=1)
                tb[leaf] = t
            else:
                t = tb[leaf]
            r = lax.dot_general(x, t, NT, preferred_element_type=f32)
            r = r[:16] + r[16:]
            outs.append(r[:, :piece] + r[:, piece:])
        block = here if side == 0 else there
        nout[pl.ds(block, 2), g] = jnp.concatenate(outs, axis=1).reshape(2, 8, n_vec * piece)

    def near_span(side, first, count):
        def body(i, carry):
            for w in range(4):
                near_group(side, first + i * 4 + w)
            return carry

        lax.fori_loop(0, count // 4, body, 0)
        for g in range(first + count // 4 * 4, first + count):
            near_group(side, g)

    edge = W // n_vec
    middle = groups - 2 * edge

    def pass_on(k):
        gathers[k].wait_recv()
        spreads[k].start()

    def take(k):
        spreads[k].wait_recv()
        split_span(1, W + chunks[k][0], chunks[k][1])

    def greet_higher():
        @pl.when(has_right)
        def _():
            pl.semaphore_wait(hello, n_leaf - 1 - li)

        for d in range(1, n_leaf):
            @pl.when(li + d < n_leaf)
            def _(d=d):
                pays[d - 1].start()

    @pl.when(li > 0)
    def _():
        greet_higher()
        one(0, 0, halos, sends, begin)

    near_span(0, edge, middle // 2)
    pass_on(0)
    pass_on(1)
    one(1, 0, halos, takes, landed)

    @pl.when(li == 0)
    def _():
        halos[0][0].start()

    both(1, halos, sends, begin)
    one(1, 0, rim_copies, takes, begin)
    def near_copy(d, part, first, count):
        u = across if d == 2 else (beside if d == 1 else n_vec - 1 - vi)
        span = pl.ds(first, count)
        return pltpu.make_async_remote_copy(
            src_ref=nout.at[u, span],
            dst_ref=near.at[vi, span],
            send_sem=near_send.at[0 if d == 1 else 2 * part + d],
            recv_sem=near_recv.at[0 if d == 1 else 2 * part + d],
            device_id=(li, u),
            device_id_type=MESH,
        )

    nears = []
    parts = []
    tail = groups - 3 * edge
    cuts = {
        tail - 2 * edge: (edge, tail - 2 * edge),
        tail - edge: (tail - edge, edge),
        0: (0, edge),
        groups - edge: (tail, 3 * edge),
    }

    def near_send_span(first, count):
        batch = [near_copy(d, len(parts), first, count) for d in (2, 3)]
        for c in batch:
            c.start()
        nears.extend(batch)
        parts.append((first, count, batch))

    def near_part(first):
        near_span(1, first, edge)
        if first in cuts:
            near_send_span(*cuts[first])


    pass_on(2)
    near_span(0, edge + middle // 2, middle - middle // 2)

    @pl.when(li == 0)
    def _():
        greet_higher()

    take(0)
    take(1)
    pass_on(3)
    one(0, 0, halos, takes, landed)
    one(0, 0, rim_copies, takes, begin)
    one(1, 0, rim_copies, takes, landed)
    split_span(0, leaves + W, W)
    near_span(0, groups - edge, edge)
    take(2)
    near_part(edge)
    ready = 2
    for first in range(2 * edge, groups - edge, edge):
        need = min(first * n_vec + 2 * W, leaves - W)
        while chunks[ready][0] + chunks[ready][1] < need:
            ready += 1
            if ready == last_chunk:
                one(0, 0, rim_copies, takes, landed)
                split_span(0, 0, W)
                near_span(0, 0, edge)
                whole = near_copy(1, 0, 0, groups)
                whole.start()
                keep = pltpu.make_async_copy(nout.at[vi], near.at[vi], near_send.at[1])
                keep.start()
                both(1, rim_copies, takes, landed)
                split_span(1, 0, W)
                split_span(1, leaves + W, W)
                near_part(0)
                gathers[last_chunk].wait_recv()
            elif ready + 1 < last_chunk:
                pass_on(ready + 1)
                both(1, halos, takes, landed)
                both(1, rim_copies, takes, begin)
            take(ready)
        near_part(first)
    near_part(groups - edge)

    for c in pays:
        c.wait_recv()
    depth = n_leaf.bit_length() - 1

    def cross_at(c):
        return n_leaf - (n_leaf >> (c - 1))

    lifts = [pay[j] for j in range(n_leaf)]
    at = 0
    starts = {}
    for c in range(1, depth):
        nodes = [
            (lifts[2 * j] + lifts[2 * j + 1]) * root_half for j in range(len(lifts) // 2)
        ]
        nodes = [swap(x) if c == 1 else x for x in nodes]
        starts[c] = at
        for j, x in enumerate(nodes):
            hx[at + j] = x
        at += len(nodes)
        if c < depth - 1:
            lifts = []
            for j, x in enumerate(nodes):
                y = dot_nn(x[:, :rank], cross_e_ref[cross_at(c) + j])
                lifts.append(jnp.concatenate([y, y], axis=1))
    z = None
    for c in range(depth - 1, 0, -1):
        node = li >> c
        sibling = node + 1 - 2 * lax.rem(node, 2)
        spot = cross_at(c) + node
        a = cross_flags_ref[spot].astype(f32)
        g = dot_nt(a * hx[starts[c] + sibling][:, :rank], cross_c_ref[spot])
        z = g if z is None else g + dot_nt(z, cross_e_ref[spot])
    sibling = li + 1 - 2 * lax.rem(li, 2)
    a = flags_ref[0, 2 * (last + 1)].astype(f32)
    x = jnp.where(low, a * pay[sibling], jnp.concatenate([z, z], axis=1))
    z = dot_nt(x, top)
    z = jnp.concatenate([z, z], axis=1)

    def down(q, parent):
        h = hp[q]
        a0 = flags_ref[0, 2 * q].astype(f32)
        a1 = flags_ref[0, 2 * q + 1].astype(f32)
        x0 = jnp.where(low, a0 * swap(h), parent)
        x1 = jnp.where(low, a1 * h, parent)
        r = dot_nt(jnp.concatenate([x0, x1], axis=0), mat_pair(q))
        zp[q] = jnp.where(low, r[:8], r[8:])

    down(last, z)
    for (a, count), (b, half) in list(zip(offs[:-1], offs[1:]))[::-1]:
        for t in range(half):
            p = zp[b + t]
            down(a + 2 * t, swap(p))
            down(a + 2 * t + 1, p)

    def far_body(i, carry):
        for w in range(8):
            t = i * 8 + w
            p = zp[t]
            s = swap(p)
            zero = jnp.zeros_like(p)
            for u in range(2):
                pair = 2 * t + u
                first, second = (p, s) if u == 0 else (s, p)
                x = jnp.concatenate(
                    [jnp.where(low, first, zero), jnp.where(low, zero, second)], axis=0
                )
                wt = basis[pl.ds(pl.multiple_of(pair * 128, 128), 128), :]
                r = dot_nn(x, wt)
                far[2 * pair] = r[:8]
                far[2 * pair + 1] = r[8:]
        return carry

    lax.fori_loop(0, leaves // 32, far_body, 0)
    keep.wait()
    whole.wait_recv()

    for c in inverses:
        c.wait_recv()
    lanes = lax.broadcasted_iota(jnp.int32, (8, size), 1)
    left = lanes < 2 * piece
    even = lax.rem(lanes // piece, 2) == 0

    def halves_of(x, y):
        moved = pltpu.roll(jnp.where(left, y, x), 2 * piece, 1)
        return jnp.where(left, x, moved), jnp.where(left, moved, y)

    def quarters_of(x, y):
        mixed = jnp.where(even, y, x)
        return (
            jnp.where(even, x, pltpu.roll(mixed, piece, 1)),
            jnp.where(even, pltpu.roll(mixed, size - piece, 1), y),
        )

    def group(g):
        p0, p1, p2, p3 = [near[v, g] for v in range(n_vec)]
        a0, a2 = halves_of(p0, p2)
        a1, a3 = halves_of(p1, p3)
        rows = quarters_of(a0, a1) + quarters_of(a2, a3)
        for u in range(n_vec):
            leaf = g * n_vec + u
            spots = jnp.broadcast_to(inverse[pl.ds(leaf, 1), :], (8, size)).astype(jnp.int32)
            out_ref[:, pl.ds(pl.multiple_of(leaf * size, size), size)] = jnp.take_along_axis(
                rows[u] + far[leaf], spots, axis=1
            )

    for batch in (parts[:-1], parts[-1:]):
        for _, _, copies in batch:
            for c in copies:
                c.wait_recv()
        for first, count, _ in batch:
            for g in range(first, first + count):
                group(g)

    for c in nears + pays + gathers + spreads + inverses + [own_copy, whole]:
        c.wait_send()
    for kind in range(2):
        both(kind, halos, sends, lambda c: c.wait_send())
        both(kind, rim_copies, takes, lambda c: c.wait_send())


def local(
    panels,
    near_tiles,
    near_cols,
    leaf_order,
    leaf_basis,
    local_mats,
    local_flags,
    cross_coupling,
    cross_transfer,
    cross_flags,
):
    rows = panels.shape[0]
    leaves, rank, size = leaf_basis.shape
    n_leaf = lax.axis_size("leaf")
    n_vec = lax.axis_size("vec")
    piece = near_tiles.shape[2]
    slots = near_tiles.shape[1]
    vmem = pl.BlockSpec(memory_space=pltpu.VMEM)
    hbm = pl.BlockSpec(memory_space=pl.ANY)
    basis2 = leaf_basis.reshape(leaves * rank, size)
    mats2 = local_mats.reshape(local_mats.shape[1] * rank, 2 * rank)
    groups = leaves // n_vec
    dma = pltpu.SemaphoreType.DMA
    return pl.pallas_call(
        functools.partial(main_kernel, n_leaf, n_vec),
        out_shape=pltpu.VMEM(panels.shape, f32),
        in_specs=[hbm] * 10,
        out_specs=vmem,
        scratch_shapes=[
            pltpu.VMEM(panels.shape, f32),
            pltpu.VMEM(leaf_order.shape, jnp.int32),
            pltpu.SMEM(near_cols.shape[::-1], jnp.int32),
            pltpu.SMEM(local_flags.shape, jnp.int32),
            pltpu.SMEM(cross_flags.shape, jnp.int32),
            pltpu.VMEM(cross_coupling.shape, f32),
            pltpu.VMEM(cross_transfer.shape, f32),
            pltpu.VMEM(near_tiles.shape, f32),
            pltpu.VMEM(basis2.shape, f32),
            pltpu.VMEM(mats2.shape, f32),
            pltpu.VMEM((n_vec, leaves + 2 * W, rows, size), f32),
            pltpu.VMEM((2, leaves + 2 * W, n_vec * rows, size), bf16),
            pltpu.VMEM((leaves, 2 * piece, slots * size), bf16),
            pltpu.VMEM((leaves // 2, rows, size), f32),
            pltpu.VMEM((leaves // 2, rows, size), f32),
            pltpu.VMEM((n_leaf, rows, 2 * rank), f32),
            pltpu.VMEM((n_leaf, rows, 2 * rank), f32),
            pltpu.VMEM((n_vec, groups, rows, size), f32),
            pltpu.VMEM((n_vec, groups, rows, size), f32),
            pltpu.VMEM((leaves, rows, size), f32),
            pltpu.VMEM((leaves, size), f32),
            dma((10,)),
            dma,
            dma,
            dma((6,)),
            dma((6,)),
            dma((6,)),
            dma((6,)),
            dma((2, 2)),
            dma((2, 2)),
            dma((2, 2)),
            dma((2, 2)),
            dma((n_leaf,)),
            dma((n_leaf,)),
            dma((10,)),
            dma((10,)),
            dma((n_vec,)),
            dma((n_vec,)),
            pltpu.SemaphoreType.REGULAR,
        ],
        compiler_params=pltpu.CompilerParams(
            collective_id=0, has_side_effects=True, vmem_limit_bytes=62 * 1024 * 1024
        ),
        name="tree",
    )(
        panels,
        leaf_order,
        near_cols.T,
        local_flags,
        cross_flags,
        cross_coupling,
        cross_transfer,
        near_tiles,
        basis2,
        mats2,
    )


def solution(mesh):
    return jax.shard_map(
        local,
        mesh=mesh,
        in_specs=(
            P("vec", "leaf"),
            P("leaf", None, "vec", None),
            P("leaf", None),
            P("leaf", None),
            P("leaf", None, None),
            P("leaf", None, None, None),
            P("leaf", None),
            P(),
            P(),
            P(),
        ),
        out_specs=P("vec", "leaf"),
        check_vma=False,
    )
```

```python
import functools
import math

import jax
import jax.numpy as jnp
from jax import lax
from jax.experimental import pallas as pl
from jax.experimental.pallas import tpu as pltpu
from jax.sharding import PartitionSpec as P

W = 8
f32 = jnp.float32
bf16 = jnp.bfloat16
root_half = 1.0 / math.sqrt(2.0)
MESH = pl.DeviceIdType.MESH
NN = (((1,), (0,)), ((), ()))
NT = (((1,), (1,)), ((), ()))


def halves(x):
    high = x.astype(bf16).astype(f32)
    return high, x - high


def stacked(x):
    return jnp.concatenate(halves(x), axis=0).astype(bf16)


def split(w):
    high = w.astype(bf16)
    return high, (w - high.astype(f32)).astype(bf16)


def dot_nt(x, w):
    rows = x.shape[0]
    lhs = stacked(x)
    r = lax.dot_general(
        jnp.concatenate([lhs, lhs], axis=1),
        jnp.concatenate(split(w), axis=1),
        NT,
        preferred_element_type=f32,
    )
    return r[:rows] + r[rows:]


def dot_nn(x, w):
    rows, cols = x.shape[0], w.shape[1]
    r = lax.dot_general(
        stacked(x), jnp.concatenate(split(w), axis=1), NN, preferred_element_type=f32
    )
    r = r[:, :cols] + r[:, cols:]
    return r[:rows] + r[rows:]


def hot_of(order_row):
    size = order_row.shape[1]
    rows = lax.broadcasted_iota(jnp.int32, (size, size), 0)
    return jnp.where(rows == order_row, 1.0, 0.0).astype(bf16)


def main_kernel(
    n_leaf,
    n_vec,
    panels_hbm,
    order_hbm,
    cols_hbm,
    flags_hbm,
    cross_flags_hbm,
    cross_c_hbm,
    cross_e_hbm,
    tiles_hbm,
    basis_hbm,
    mats_hbm,
    out_ref,
    panels,
    order,
    cols_ref,
    flags_ref,
    cross_flags_ref,
    cross_c_ref,
    cross_e_ref,
    tiles,
    basis,
    mats,
    ext,
    xs,
    tb,
    hp,
    zp,
    pay,
    hx,
    nout,
    near,
    far,
    inverse,
    load_sem,
    own_send,
    own_recv,
    gather_send,
    gather_recv,
    spread_send,
    spread_recv,
    halo_send,
    halo_recv,
    rim_send,
    rim_recv,
    pay_send,
    pay_recv,
    near_send,
    near_recv,
    inv_send,
    inv_recv,
    hello,
):
    leaves, size = order.shape
    rank = 64
    slots = tiles.shape[1]
    piece = tiles.shape[2]
    groups = leaves // n_vec
    li = lax.axis_index("leaf")
    vi = lax.axis_index("vec")
    loads = [
        pltpu.make_async_copy(src, dst, load_sem.at[i])
        for i, (src, dst) in enumerate(
            [
                (panels_hbm, panels),
                (order_hbm, order),
                (basis_hbm, basis),
                (mats_hbm, mats),
                (tiles_hbm, tiles),
                (cols_hbm, cols_ref),
                (flags_hbm, flags_ref),
                (cross_flags_hbm, cross_flags_ref),
                (cross_c_hbm, cross_c_ref),
                (cross_e_hbm, cross_e_ref),
            ]
        )
    ]
    load_p, load_o, load_b, load_m, load_t = loads[:5]
    small = loads[5:]
    for c in loads[:3]:
        c.start()

    barrier = pltpu.get_barrier_semaphore()
    for d in range(1, n_vec):
        pl.semaphore_signal(
            barrier, inc=1, device_id=(li, lax.rem(vi + d, n_vec)), device_id_type=MESH
        )
    for d in range(1, n_leaf):
        @pl.when(li + d < n_leaf)
        def _(d=d):
            pl.semaphore_signal(
                barrier, inc=1, device_id=(lax.rem(li + d, n_leaf), vi), device_id_type=MESH
            )
    load_m.start()
    for c in small:
        c.start()

    assert n_vec == 4
    beside = vi + 1 - 2 * lax.rem(vi, 2)
    across = lax.rem(vi + 2, n_vec)
    here = vi - lax.rem(vi, 2)
    there = lax.rem(here + 2, n_vec)
    has_left = li > 0
    has_right = li < n_leaf - 1
    chunks = [(0, W), (leaves - W, W)]
    at = W
    while at < leaves - W:
        wide = 2 * W if leaves - W - at > 2 * W else W
        chunks.append((at, wide))
        at += wide

    own_copy = pltpu.make_async_remote_copy(
        src_ref=ext.at[vi, pl.ds(W, leaves)],
        dst_ref=ext.at[vi, pl.ds(W, leaves)],
        send_sem=own_send,
        recv_sem=own_recv,
        device_id=(li, beside),
        device_id_type=MESH,
    )

    def gather_copy(k, target):
        sems = (gather_send, gather_recv) if target is across else (spread_send, spread_recv)
        block = ext.at[vi, pl.ds(W + chunks[k][0], chunks[k][1])]
        return pltpu.make_async_remote_copy(
            src_ref=block,
            dst_ref=block,
            send_sem=sems[0].at[k],
            recv_sem=sems[1].at[k],
            device_id=(li, target),
            device_id_type=MESH,
        )

    def spread_copy(k):
        block = ext.at[across, pl.ds(W + chunks[k][0], chunks[k][1])]
        return pltpu.make_async_remote_copy(
            src_ref=block,
            dst_ref=block,
            send_sem=spread_send.at[k],
            recv_sem=spread_recv.at[k],
            device_id=(li, beside),
            device_id_type=MESH,
        )

    rims = (0, leaves + W)
    sends = (has_right, has_left)
    takes = (has_left, has_right)

    def halo_copy(side, kind):
        vec = vi if kind == 0 else across
        target = jnp.minimum(li + 1, n_leaf - 1) if side == 0 else jnp.maximum(li - 1, 0)
        return pltpu.make_async_remote_copy(
            src_ref=ext.at[vec, pl.ds(leaves if side == 0 else W, W)],
            dst_ref=ext.at[vec, pl.ds(rims[side], W)],
            send_sem=halo_send.at[side, kind],
            recv_sem=halo_recv.at[side, kind],
            device_id=(target, vi),
            device_id_type=MESH,
        )

    def rim_copy(side, kind):
        block = ext.at[vi if kind == 0 else across, pl.ds(rims[side], W)]
        return pltpu.make_async_remote_copy(
            src_ref=block,
            dst_ref=block,
            send_sem=rim_send.at[side, kind],
            recv_sem=rim_recv.at[side, kind],
            device_id=(li, beside),
            device_id_type=MESH,
        )

    last_chunk = len(chunks) - 1
    gathers = [gather_copy(k, across) for k in range(len(chunks))]
    spreads = [spread_copy(k) for k in range(last_chunk - 1)]
    spreads += [gather_copy(k, n_vec - 1 - vi) for k in (last_chunk - 1, last_chunk)]
    halos = [[halo_copy(side, kind) for side in range(2)] for kind in range(2)]
    rim_copies = [[rim_copy(side, kind) for side in range(2)] for kind in range(2)]

    def begin(c):
        c.start()

    def landed(c):
        c.wait_recv()

    def one(side, kind, copies, conditions, act):
        @pl.when(conditions[side])
        def _():
            act(copies[kind][side])

    def both(kind, copies, conditions, act):
        for side in range(2):
            one(side, kind, copies, conditions, act)

    lane = lax.broadcasted_iota(jnp.int32, (8, 2 * rank), 1)
    low = lane < rank

    def swap(x):
        return pltpu.roll(x, rank, 1)

    load_p.wait()
    load_o.wait()

    def order_span(first, count):
        for leaf in range(first, first + count):
            x = panels[:, leaf * size : (leaf + 1) * size]
            spots = jnp.broadcast_to(order[pl.ds(leaf, 1), :], x.shape)
            ext[vi, W + leaf] = jnp.take_along_axis(x, spots, axis=1)

    early = (li == 0) & (here == 0)

    def greet_lower():
        own_copy.start()
        for d in range(1, n_leaf):
            @pl.when(li + d >= n_leaf)
            def _(d=d):
                pl.semaphore_signal(
                    hello, inc=1, device_id=(lax.rem(li + d, n_leaf), vi), device_id_type=MESH
                )

    @pl.when(jnp.logical_not(early))
    def _():
        order_span(*chunks[0])
        order_span(*chunks[1])
        pl.semaphore_wait(barrier, n_vec - 1 + li)
        gathers[0].start()
        gathers[1].start()
        one(1, 0, halos, sends, begin)
        for k in range(2, len(chunks)):
            order_span(*chunks[k])
            gathers[k].start()
            if k >= last_chunk - 1:
                spreads[k].start()
        greet_lower()

    @pl.when(early)
    def _():
        for k in range(len(chunks)):
            order_span(*chunks[k])
        pl.semaphore_wait(barrier, n_vec - 1 + li)
        for c in gathers[:-1] + spreads[last_chunk - 1 : last_chunk] + gathers[-1:] + spreads[last_chunk:]:
            c.start()
        one(1, 0, halos, sends, begin)
        greet_lower()

    load_b.wait()
    load_t.start()

    def skel_body(i, carry):
        for w in range(8):
            t = i * 8 + w
            sums = []
            for u in range(2):
                pair = t * 2 + u
                x = ext[vi, pl.ds(W + pair * 2, 2)].reshape(16, 128)
                wt = basis[pl.ds(pl.multiple_of(pair * 128, 128), 128), :]
                r = dot_nt(x, wt)
                sums.append((r[:8], r[8:]))
            even = sums[0][0] + swap(sums[0][1])
            odd = swap(sums[1][0]) + sums[1][1]
            hp[t] = jnp.where(low, even, odd) * root_half
        return carry

    lax.fori_loop(0, leaves // 32, skel_body, 0)

    load_m.wait()

    def mat_pair(q):
        return mats[pl.ds(pl.multiple_of(q * 128, 128), 128), :]

    def up(off, nxt, t):
        r0 = dot_nn(hp[off + 2 * t], mat_pair(off + 2 * t))
        r1 = dot_nn(hp[off + 2 * t + 1], mat_pair(off + 2 * t + 1))
        hp[nxt + t] = jnp.where(low, swap(r0), r1) * root_half

    pairs = leaves // 4
    offs = []
    off = 0
    while pairs >= 1:
        offs.append((off, pairs))
        off += pairs
        pairs //= 2
    for (a, count), (b, half) in zip(offs[:-1], offs[1:]):
        for t in range(half):
            up(a, b, t)
    last = offs[-1][0]
    r = dot_nn(hp[last], mat_pair(last))
    skel = swap(r) * root_half
    top = mats[pl.ds((last + 1) * 128, rank), :]
    lift = dot_nn(skel[:, :rank], top)
    pay[li] = jnp.where(low, skel, lift)

    def pay_copy(d):
        return pltpu.make_async_remote_copy(
            src_ref=pay.at[li],
            dst_ref=pay.at[li],
            send_sem=pay_send.at[d],
            recv_sem=pay_recv.at[n_leaf - d],
            device_id=(lax.rem(li + d, n_leaf), vi),
            device_id_type=MESH,
        )

    pays = [pay_copy(d) for d in range(1, n_leaf)]

    for d in range(1, n_leaf):
        @pl.when(li + d >= n_leaf)
        def _(d=d):
            pays[d - 1].start()

    counts = lax.broadcasted_iota(jnp.int32, (8, size), 1).astype(f32)
    spot_row = lax.broadcasted_iota(jnp.int32, (8, size), 0)
    share = leaves // n_vec

    def picked(w):
        return jnp.where(spot_row == w, counts, 0.0)

    for first in range(0, share, 8):
        start = vi * share + first
        rows = order[pl.ds(pl.multiple_of(start, 8), 8), :]
        total = None
        for w in range(0, 8, 2):
            lhs = jnp.concatenate([picked(w), picked(w + 1)], axis=1).astype(bf16)
            hot = jnp.concatenate([hot_of(rows[w : w + 1]), hot_of(rows[w + 1 : w + 2])], axis=1)
            r = lax.dot_general(lhs, hot, NT, preferred_element_type=f32)
            total = r if total is None else total + r
        inverse[pl.ds(pl.multiple_of(start, 8), 8), :] = total

    def inverse_copy(d):
        block = inverse.at[pl.ds(pl.multiple_of(vi * share, 8), share)]
        return pltpu.make_async_remote_copy(
            src_ref=block,
            dst_ref=block,
            send_sem=inv_send.at[d],
            recv_sem=inv_recv.at[n_vec - d],
            device_id=(li, lax.rem(vi + d, n_vec)),
            device_id_type=MESH,
        )

    inverses = [inverse_copy(d) for d in range(1, n_vec)]
    for c in inverses:
        c.start()

    def split_span(side, first, count):
        block = here if side == 0 else there

        def body(i, carry):
            for w in range(8):
                e = first + i * 8 + w
                x = ext[pl.ds(block, 2), e].reshape(16, 128)
                xs[side, e] = stacked(x)
            return carry

        lax.fori_loop(0, count // 8, body, 0)

    for c in small:
        c.wait()
    own_copy.wait_recv()
    split_span(0, W, leaves)
    load_t.wait()
    base = li * leaves - W

    def place(leaf, n):
        return jnp.clip(cols_ref[n, leaf] - base, 0, leaves + 2 * W - 1)

    def near_group(side, g):
        outs = []
        for w in range(n_vec):
            leaf = g * n_vec + w
            x = jnp.concatenate([xs[side, place(leaf, n)] for n in range(slots)], axis=1)
            if side == 0:
                t = jnp.concatenate([stacked(tiles[leaf, n]) for n in range(slots)], axis=1)
                tb[leaf] = t
            else:
                t = tb[leaf]
            r = lax.dot_general(x, t, NT, preferred_element_type=f32)
            r = r[:16] + r[16:]
            outs.append(r[:, :piece] + r[:, piece:])
        block = here if side == 0 else there
        nout[pl.ds(block, 2), g] = jnp.concatenate(outs, axis=1).reshape(2, 8, n_vec * piece)

    def near_span(side, first, count):
        def body(i, carry):
            for w in range(4):
                near_group(side, first + i * 4 + w)
            return carry

        lax.fori_loop(0, count // 4, body, 0)
        for g in range(first + count // 4 * 4, first + count):
            near_group(side, g)

    edge = W // n_vec
    middle = groups - 2 * edge

    def pass_on(k):
        gathers[k].wait_recv()
        spreads[k].start()

    def take(k):
        spreads[k].wait_recv()
        split_span(1, W + chunks[k][0], chunks[k][1])

    def greet_higher():
        @pl.when(has_right)
        def _():
            pl.semaphore_wait(hello, n_leaf - 1 - li)

        for d in range(1, n_leaf):
            @pl.when(li + d < n_leaf)
            def _(d=d):
                pays[d - 1].start()

    @pl.when(li > 0)
    def _():
        greet_higher()
        one(0, 0, halos, sends, begin)

    near_span(0, edge, middle // 2)
    pass_on(0)
    pass_on(1)
    one(1, 0, halos, takes, landed)

    @pl.when(li == 0)
    def _():
        halos[0][0].start()

    both(1, halos, sends, begin)
    one(1, 0, rim_copies, takes, begin)
    def near_copy(d, part, first, count):
        u = across if d == 2 else (beside if d == 1 else n_vec - 1 - vi)
        span = pl.ds(first, count)
        return pltpu.make_async_remote_copy(
            src_ref=nout.at[u, span],
            dst_ref=near.at[vi, span],
            send_sem=near_send.at[0 if d == 1 else 2 * part + d],
            recv_sem=near_recv.at[0 if d == 1 else 2 * part + d],
            device_id=(li, u),
            device_id_type=MESH,
        )

    nears = []
    parts = []
    tail = groups - 3 * edge
    cuts = {
        tail - 2 * edge: (edge, tail - 2 * edge),
        tail - edge: (tail - edge, edge),
        0: (0, edge),
        groups - edge: (tail, 3 * edge),
    }

    def near_send_span(first, count):
        batch = [near_copy(d, len(parts), first, count) for d in (2, 3)]
        for c in batch:
            c.start()
        nears.extend(batch)
        parts.append((first, count, batch))

    def near_part(first):
        near_span(1, first, edge)
        if first in cuts:
            near_send_span(*cuts[first])


    pass_on(2)
    near_span(0, edge + middle // 2, middle - middle // 2)

    @pl.when(li == 0)
    def _():
        greet_higher()

    take(0)
    take(1)
    pass_on(3)
    one(0, 0, halos, takes, landed)
    one(0, 0, rim_copies, takes, begin)
    one(1, 0, rim_copies, takes, landed)
    split_span(0, leaves + W, W)
    near_span(0, groups - edge, edge)
    take(2)
    near_part(edge)
    ready = 2
    for first in range(2 * edge, groups - edge, edge):
        need = min(first * n_vec + 2 * W, leaves - W)
        while chunks[ready][0] + chunks[ready][1] < need:
            ready += 1
            if ready == last_chunk:
                one(0, 0, rim_copies, takes, landed)
                split_span(0, 0, W)
                near_span(0, 0, edge)
                whole = near_copy(1, 0, 0, groups)
                whole.start()
                keep = pltpu.make_async_copy(nout.at[vi], near.at[vi], near_send.at[1])
                keep.start()
                both(1, rim_copies, takes, landed)
                split_span(1, 0, W)
                split_span(1, leaves + W, W)
                near_part(0)
                gathers[last_chunk].wait_recv()
            elif ready + 1 < last_chunk:
                both(1, halos, takes, landed)
                both(1, rim_copies, takes, begin)
            if ready == last_chunk - 1:
                gathers[ready].wait_recv()
            take(ready)
        near_part(first)
    near_part(groups - edge)

    for c in pays:
        c.wait_recv()
    depth = n_leaf.bit_length() - 1

    def cross_at(c):
        return n_leaf - (n_leaf >> (c - 1))

    lifts = [pay[j] for j in range(n_leaf)]
    at = 0
    starts = {}
    for c in range(1, depth):
        nodes = [
            (lifts[2 * j] + lifts[2 * j + 1]) * root_half for j in range(len(lifts) // 2)
        ]
        nodes = [swap(x) if c == 1 else x for x in nodes]
        starts[c] = at
        for j, x in enumerate(nodes):
            hx[at + j] = x
        at += len(nodes)
        if c < depth - 1:
            lifts = []
            for j, x in enumerate(nodes):
                y = dot_nn(x[:, :rank], cross_e_ref[cross_at(c) + j])
                lifts.append(jnp.concatenate([y, y], axis=1))
    z = None
    for c in range(depth - 1, 0, -1):
        node = li >> c
        sibling = node + 1 - 2 * lax.rem(node, 2)
        spot = cross_at(c) + node
        a = cross_flags_ref[spot].astype(f32)
        g = dot_nt(a * hx[starts[c] + sibling][:, :rank], cross_c_ref[spot])
        z = g if z is None else g + dot_nt(z, cross_e_ref[spot])
    sibling = li + 1 - 2 * lax.rem(li, 2)
    a = flags_ref[0, 2 * (last + 1)].astype(f32)
    x = jnp.where(low, a * pay[sibling], jnp.concatenate([z, z], axis=1))
    z = dot_nt(x, top)
    z = jnp.concatenate([z, z], axis=1)

    def down(q, parent):
        h = hp[q]
        a0 = flags_ref[0, 2 * q].astype(f32)
        a1 = flags_ref[0, 2 * q + 1].astype(f32)
        x0 = jnp.where(low, a0 * swap(h), parent)
        x1 = jnp.where(low, a1 * h, parent)
        r = dot_nt(jnp.concatenate([x0, x1], axis=0), mat_pair(q))
        zp[q] = jnp.where(low, r[:8], r[8:])

    down(last, z)
    for (a, count), (b, half) in list(zip(offs[:-1], offs[1:]))[::-1]:
        for t in range(half):
            p = zp[b + t]
            down(a + 2 * t, swap(p))
            down(a + 2 * t + 1, p)

    def far_body(i, carry):
        for w in range(8):
            t = i * 8 + w
            p = zp[t]
            s = swap(p)
            zero = jnp.zeros_like(p)
            for u in range(2):
                pair = 2 * t + u
                first, second = (p, s) if u == 0 else (s, p)
                x = jnp.concatenate(
                    [jnp.where(low, first, zero), jnp.where(low, zero, second)], axis=0
                )
                wt = basis[pl.ds(pl.multiple_of(pair * 128, 128), 128), :]
                r = dot_nn(x, wt)
                far[2 * pair] = r[:8]
                far[2 * pair + 1] = r[8:]
        return carry

    lax.fori_loop(0, leaves // 32, far_body, 0)
    keep.wait()
    whole.wait_recv()

    for c in inverses:
        c.wait_recv()
    lanes = lax.broadcasted_iota(jnp.int32, (8, size), 1)
    left = lanes < 2 * piece
    even = lax.rem(lanes // piece, 2) == 0

    def halves_of(x, y):
        moved = pltpu.roll(jnp.where(left, y, x), 2 * piece, 1)
        return jnp.where(left, x, moved), jnp.where(left, moved, y)

    def quarters_of(x, y):
        mixed = jnp.where(even, y, x)
        return (
            jnp.where(even, x, pltpu.roll(mixed, piece, 1)),
            jnp.where(even, pltpu.roll(mixed, size - piece, 1), y),
        )

    def group(g):
        p0, p1, p2, p3 = [near[v, g] for v in range(n_vec)]
        a0, a2 = halves_of(p0, p2)
        a1, a3 = halves_of(p1, p3)
        rows = quarters_of(a0, a1) + quarters_of(a2, a3)
        for u in range(n_vec):
            leaf = g * n_vec + u
            spots = jnp.broadcast_to(inverse[pl.ds(leaf, 1), :], (8, size)).astype(jnp.int32)
            out_ref[:, pl.ds(pl.multiple_of(leaf * size, size), size)] = jnp.take_along_axis(
                rows[u] + far[leaf], spots, axis=1
            )

    for batch in (parts[:-1], parts[-1:]):
        for _, _, copies in batch:
            for c in copies:
                c.wait_recv()
        for first, count, _ in batch:
            for g in range(first, first + count):
                group(g)

    for c in nears + pays + gathers + spreads + inverses + [own_copy, whole]:
        c.wait_send()
    for kind in range(2):
        both(kind, halos, sends, lambda c: c.wait_send())
        both(kind, rim_copies, takes, lambda c: c.wait_send())


def local(
    panels,
    near_tiles,
    near_cols,
    leaf_order,
    leaf_basis,
    local_mats,
    local_flags,
    cross_coupling,
    cross_transfer,
    cross_flags,
):
    rows = panels.shape[0]
    leaves, rank, size = leaf_basis.shape
    n_leaf = lax.axis_size("leaf")
    n_vec = lax.axis_size("vec")
    piece = near_tiles.shape[2]
    slots = near_tiles.shape[1]
    vmem = pl.BlockSpec(memory_space=pltpu.VMEM)
    hbm = pl.BlockSpec(memory_space=pl.ANY)
    basis2 = leaf_basis.reshape(leaves * rank, size)
    mats2 = local_mats.reshape(local_mats.shape[1] * rank, 2 * rank)
    groups = leaves // n_vec
    dma = pltpu.SemaphoreType.DMA
    return pl.pallas_call(
        functools.partial(main_kernel, n_leaf, n_vec),
        out_shape=pltpu.VMEM(panels.shape, f32),
        in_specs=[hbm] * 10,
        out_specs=vmem,
        scratch_shapes=[
            pltpu.VMEM(panels.shape, f32),
            pltpu.VMEM(leaf_order.shape, jnp.int32),
            pltpu.SMEM(near_cols.shape[::-1], jnp.int32),
            pltpu.SMEM(local_flags.shape, jnp.int32),
            pltpu.SMEM(cross_flags.shape, jnp.int32),
            pltpu.VMEM(cross_coupling.shape, f32),
            pltpu.VMEM(cross_transfer.shape, f32),
            pltpu.VMEM(near_tiles.shape, f32),
            pltpu.VMEM(basis2.shape, f32),
            pltpu.VMEM(mats2.shape, f32),
            pltpu.VMEM((n_vec, leaves + 2 * W, rows, size), f32),
            pltpu.VMEM((2, leaves + 2 * W, n_vec * rows, size), bf16),
            pltpu.VMEM((leaves, 2 * piece, slots * size), bf16),
            pltpu.VMEM((leaves // 2, rows, size), f32),
            pltpu.VMEM((leaves // 2, rows, size), f32),
            pltpu.VMEM((n_leaf, rows, 2 * rank), f32),
            pltpu.VMEM((n_leaf, rows, 2 * rank), f32),
            pltpu.VMEM((n_vec, groups, rows, size), f32),
            pltpu.VMEM((n_vec, groups, rows, size), f32),
            pltpu.VMEM((leaves, rows, size), f32),
            pltpu.VMEM((leaves, size), f32),
            dma((10,)),
            dma,
            dma,
            dma((6,)),
            dma((6,)),
            dma((6,)),
            dma((6,)),
            dma((2, 2)),
            dma((2, 2)),
            dma((2, 2)),
            dma((2, 2)),
            dma((n_leaf,)),
            dma((n_leaf,)),
            dma((10,)),
            dma((10,)),
            dma((n_vec,)),
            dma((n_vec,)),
            pltpu.SemaphoreType.REGULAR,
        ],
        compiler_params=pltpu.CompilerParams(
            collective_id=0, has_side_effects=True, vmem_limit_bytes=62 * 1024 * 1024
        ),
        name="tree",
    )(
        panels,
        leaf_order,
        near_cols.T,
        local_flags,
        cross_flags,
        cross_coupling,
        cross_transfer,
        near_tiles,
        basis2,
        mats2,
    )


def solution(mesh):
    return jax.shard_map(
        local,
        mesh=mesh,
        in_specs=(
            P("vec", "leaf"),
            P("leaf", None, "vec", None),
            P("leaf", None),
            P("leaf", None),
            P("leaf", None, None),
            P("leaf", None, None, None),
            P("leaf", None),
            P(),
            P(),
            P(),
        ),
        out_specs=P("vec", "leaf"),
        check_vma=False,
    )
```
